32 devices in a mesh: shard: 2 (over core), context: 4 (over y, x), tensor: 4 (over z).
Axes of the slice: x: 2, y: 2, z: 4, core: 2. Of those that a mesh axis runs over, the one named last changes fastest.
Arguments:
- tokens: bfloat16 [2, 4096, 2048], P('shard', 'context'), may hold values from -6 to 6
- segments: int32 [2, 4096], P('shard', 'context'), may hold values from 0 to 11, never falling along the last dimension, each value on 1 to 2048 neighbouring positions
- cotangent: bfloat16 [2, 4096, 2048], P('shard', 'context'), may hold values from -6 to 6
- norm_attn: bfloat16 [2048], P(('shard', 'context')), may hold values from 0.5 to 1.5
- w_query: bfloat16 [2048, 2048], P(('shard', 'context'), 'tensor'), may hold values from -0.125 to 0.125
- key_matrix: bfloat16 [2048, 1024], P(('shard', 'context'), 'tensor'), may hold values from -0.125 to 0.125
- value_matrix: bfloat16 [2048, 1024], P(('shard', 'context'), 'tensor'), may hold values from -0.125 to 0.125
- w_headgate: bfloat16 [2048, 16], P(('shard', 'context'), 'tensor'), may hold values from -0.125 to 0.125
- query_gain: bfloat16 [128], P(('shard', 'context')), may hold values from 0.5 to 1.5
- key_gain: bfloat16 [128], P(('shard', 'context')), may hold values from 0.5 to 1.5
- w_out: bfloat16 [2048, 2048], P(('shard', 'context'), 'tensor'), may hold values from -0.75 to 0.75
- norm_ffn: bfloat16 [2048], P(('shard', 'context')), may hold values from 0.5 to 1.5
- w_gate: bfloat16 [2048, 6144], P(('shard', 'context'), 'tensor'), may hold values from -0.125 to 0.125
- w_up: bfloat16 [2048, 6144], P(('shard', 'context'), 'tensor'), may hold values from -0.125 to 0.125
- w_down: bfloat16 [2048, 6144], P(('shard', 'context'), 'tensor'), may hold values from -0.078125 to 0.078125
Outputs:
- layer_out: bfloat16 [2, 4096, 2048], P('shard', 'context')
- tokens_grad: float32 [2, 4096, 2048], P('shard', 'context')
- grad_norm_attn: float32 [2048], P(('shard', 'context'))
- grad_query: float32 [2048, 2048], P(('shard', 'context'), 'tensor')
- grad_key: float32 [2048, 1024], P(('shard', 'context'), 'tensor')
- grad_value: float32 [2048, 1024], P(('shard', 'context'), 'tensor')
- grad_headgate: float32 [2048, 16], P(('shard', 'context'), 'tensor')
- grad_query_gain: float32 [128], P(('shard', 'context'))
- grad_key_gain: float32 [128], P(('shard', 'context'))
- grad_out: float32 [2048, 2048], P(('shard', 'context'), 'tensor')
- grad_norm_ffn: float32 [2048], P(('shard', 'context'))
- grad_gate: float32 [2048, 6144], P(('shard', 'context'), 'tensor')
- grad_up: float32 [2048, 6144], P(('shard', 'context'), 'tensor')
- grad_down: float32 [2048, 6144], P(('shard', 'context'), 'tensor')
The draws below stay inside these ranges and needn't reach their ends.
Inputs may be any that keep to these rules, and one draw needn't show every extreme that they name: `segments`: each sequence's document ids never fall along its positions; a document holds 1 to 2048 tokens.
All inputs are finite; a program needn't handle non-finite values.
Results may differ from the reference program's by a relative error of at most 0.025.
Values may be sent and summed in bfloat16 or wider, within the bound.
No kernel may reach another device: no remote copies, remote signals or barrier semaphores. Data moves between devices by JAX's collectives and lax.ppermute only.
A program may use at most 384 MiB of HBM per device.

```python
import math
import jax
import jax.numpy as jnp
import numpy as np
from jax import lax

MODEL_DIM = 2048
QUERY_HEADS = 16
KEY_VALUE_HEADS = 8
HEAD_DIM = 128
FF = 6144
LENGTH = 4096
DOCS = 12
BATCH = 2


def block_levels(key, shape, pieces, low, largest):
    gain = 1.0
    for position, blocks in pieces:
        heights = jax.random.uniform(jax.random.fold_in(jax.random.fold_in(key, 6), position), (blocks,), jnp.float32, low / len(pieces), largest / len(pieces))
        gain = gain * jnp.repeat(jnp.exp(heights), shape[position] // blocks).reshape((-1,) + (1,) * (len(shape) - 1 - position))
    return gain


def length_profile(number_of, total, limit, skew):
    weights = [(1 << 20) // math.isqrt(grade ** skew) + 1 for grade in range(2, number_of + 1)]
    surplus, counts = total - limit - (number_of - 1), [1] * (number_of - 1)
    while surplus > 0:
        movable = [i for i in range(number_of - 1) if counts[i] < limit]
        mass, remaining = sum([weights[i] for i in movable]), surplus
        for i in movable:
            addition = min(limit - counts[i], max(1, remaining * weights[i] // mass), surplus)
            counts[i] = counts[i] + addition
            surplus = surplus - addition
    return np.array([limit] + counts)


def ragged_sizes(stream_key, count, total, most, lean):
    if count == 2:
        one = jax.random.randint(stream_key, (), max(1, total - most), min(most, total - 1) + 1)
        return jnp.stack([one, total - one])
    lengths = jnp.asarray(length_profile(count, total, most, lean), jnp.int32)
    pairs = (count - 1) // 2
    donor, taker = lengths[1:1 + 2 * pairs:2], lengths[2:2 + 2 * pairs:2]
    slack = jnp.minimum(donor - 1, most - taker)
    shifted = jax.random.randint(jax.random.fold_in(stream_key, 1), (pairs,), 0, 1 << 20) % (slack + 1)
    lengths = lengths.at[1:1 + 2 * pairs:2].set(donor - shifted).at[2:2 + 2 * pairs:2].set(taker + shifted)
    return lengths[jax.random.permutation(jax.random.fold_in(stream_key, 2), count)]


def bell_draw(rng, shape, deviation, bound, split=(), kind=jnp.bfloat16):
    drawn = deviation * jax.random.normal(rng, shape, jnp.float32)
    if split:
        drawn = drawn * block_levels(rng, shape, split, -0.22, 0.18)
    return jnp.clip(drawn, -bound, bound).astype(kind)


def setup_inputs(seed: int = 0) -> dict:
    key_of = jax.random.split(jax.random.key(seed), 16)
    tokens = bell_draw(key_of[0], (BATCH, LENGTH, MODEL_DIM), 1.0, 6.0, ((0, 2), (1, 4)))
    segments = jax.vmap(lambda own: jnp.searchsorted(jnp.cumsum(ragged_sizes(own, DOCS, LENGTH, LENGTH // 2, 2)), jnp.arange(LENGTH), side="right"))(jax.random.split(key_of[1], BATCH)).reshape((BATCH, LENGTH)).astype(jnp.int32)
    cotangent = bell_draw(key_of[2], (BATCH, LENGTH, MODEL_DIM), 1.0, 6.0, ((0, 2), (1, 4)))
    norm_attn = jnp.clip(1.0 + 0.1 * jax.random.normal(key_of[3], (MODEL_DIM,), jnp.float32), 0.5, 1.5).astype(jnp.bfloat16)
    w_query = bell_draw(key_of[4], (MODEL_DIM, QUERY_HEADS * HEAD_DIM), MODEL_DIM ** -0.5, 0.125, ((0, 8), (1, 4)))
    key_matrix = bell_draw(key_of[5], (MODEL_DIM, KEY_VALUE_HEADS * HEAD_DIM), MODEL_DIM ** -0.5, 0.125, ((0, 8), (1, 4)))
    value_matrix = bell_draw(key_of[6], (MODEL_DIM, KEY_VALUE_HEADS * HEAD_DIM), MODEL_DIM ** -0.5, 0.125, ((0, 8), (1, 4)))
    w_headgate = bell_draw(key_of[7], (MODEL_DIM, QUERY_HEADS), MODEL_DIM ** -0.5, 0.125, ((0, 8), (1, 4)))
    query_gain = jnp.clip(1.0 + 0.1 * jax.random.normal(key_of[8], (HEAD_DIM,), jnp.float32), 0.5, 1.5).astype(jnp.bfloat16)
    key_gain = jnp.clip(1.0 + 0.1 * jax.random.normal(key_of[9], (HEAD_DIM,), jnp.float32), 0.5, 1.5).astype(jnp.bfloat16)
    w_out = bell_draw(key_of[10], (MODEL_DIM, QUERY_HEADS * HEAD_DIM), (QUERY_HEADS * HEAD_DIM // 32) ** -0.5, 0.75, ((0, 8), (1, 4)))
    norm_ffn = jnp.clip(1.0 + 0.1 * jax.random.normal(key_of[11], (MODEL_DIM,), jnp.float32), 0.5, 1.5).astype(jnp.bfloat16)
    w_gate = bell_draw(key_of[12], (MODEL_DIM, FF), MODEL_DIM ** -0.5, 0.125, ((0, 8), (1, 4)))
    w_up = bell_draw(key_of[13], (MODEL_DIM, FF), MODEL_DIM ** -0.5, 0.125, ((0, 8), (1, 4)))
    w_down = bell_draw(key_of[14], (MODEL_DIM, FF), FF ** -0.5, 0.078125, ((0, 8), (1, 4)))
    return dict(tokens=tokens, segments=segments, cotangent=cotangent, norm_attn=norm_attn, w_query=w_query, key_matrix=key_matrix, value_matrix=value_matrix, w_headgate=w_headgate, query_gain=query_gain, key_gain=key_gain, w_out=w_out, norm_ffn=norm_ffn, w_gate=w_gate, w_up=w_up, w_down=w_down)


EPS = 1e-06
THETA = 1000000.0
NEGATIVE = -1e+30
HIGH = lax.Precision.HIGHEST

@jax.custom_vjp
def reduced_precision(v):
    return lax.optimization_barrier(v.astype(jnp.bfloat16)).astype(jnp.float32)

@jax.custom_vjp
def reduced_backward(v):
    return v

def low_keep(v):
    return (reduced_precision(v), None)

def low_pass(kept, grad):
    return (grad,)

def back_keep(v):
    return (v, None)

def back_low(kept, grad):
    return (reduced_precision(grad),)
reduced_precision.defvjp(low_keep, low_pass)
reduced_backward.defvjp(back_keep, back_low)

def rotate(value_vectors):
    middle = value_vectors.shape[-1] // 2
    return jnp.concatenate([-value_vectors[..., middle:], value_vectors[..., :middle]], -1)

def rope_tables(positions, head_size):
    middle = head_size // 2
    frequency = jnp.exp(jnp.arange(middle, dtype=jnp.float32) * (-2.0 * math.log(THETA) / head_size))
    angles = positions[..., None] * frequency
    angles = jnp.concatenate([angles, angles], -1)
    return (jnp.cos(angles), jnp.sin(angles))

def doc_positions(seg_row):
    span_length = seg_row.shape[0]
    before = lax.optimization_barrier(jnp.sum(seg_row[None, :] < seg_row[:, None], axis=1, dtype=jnp.int32))
    return (jnp.arange(span_length, dtype=jnp.int32) - before).astype(jnp.float32)

def matrix_multiply(operand, weight):
    return jnp.dot(operand, weight, precision=HIGH)

def matmul_t(operand, weight):
    return jnp.dot(operand, weight.T, precision=HIGH)

def attention(query_rotated, k_rot, value_vectors, seg_row):
    span_length = seg_row.shape[0]
    rows_per_block = math.gcd(span_length, 512)
    item_count = span_length // rows_per_block
    query_group_width = QUERY_HEADS // KEY_VALUE_HEADS
    query_block_list = query_rotated.reshape(item_count, rows_per_block, KEY_VALUE_HEADS, query_group_width, HEAD_DIM)
    seg_blocks = seg_row.reshape(item_count, rows_per_block)
    starts = jnp.arange(item_count, dtype=jnp.int32) * rows_per_block
    key_pos = jnp.arange(span_length, dtype=jnp.int32)
    inv_root = 1.0 / math.sqrt(HEAD_DIM)

    def attend_block(block_items):
        queries, query_ids, start_row = block_items
        scores = reduced_backward(jnp.einsum('cngd,rnd->ngcr', queries, k_rot, precision=HIGH) * inv_root)
        query_pos = start_row + jnp.arange(rows_per_block, dtype=jnp.int32)
        allowed = (query_ids[:, None] == seg_row[None, :]) & (key_pos[None, :] <= query_pos[:, None])
        masked = jnp.where(allowed, scores, NEGATIVE)
        top_row = lax.optimization_barrier(jnp.max(masked, -1, keepdims=True))
        exponent = jnp.exp(masked - top_row)
        weights = exponent / lax.optimization_barrier(jnp.sum(exponent, -1, keepdims=True))
        return jnp.einsum('ngcr,rnd->cngd', reduced_precision(weights), value_vectors, precision=HIGH)
    result = lax.map(jax.checkpoint(attend_block), (query_block_list, seg_blocks, starts))
    return result.reshape(span_length, QUERY_HEADS, HEAD_DIM)

def block_forward(resid_in, seg_row, gain_attn, query_full, complete_keys, complete_values, headgate_full, gain_query, gain_key, out_full, gain_ffn, gate_full, up_full, down_full):
    span_length = resid_in.shape[0]
    cos_table, sin_table = rope_tables(doc_positions(seg_row), HEAD_DIM)
    cos_heads = cos_table[:, None, :]
    sin_heads = sin_table[:, None, :]
    scale1 = lax.rsqrt(lax.optimization_barrier(jnp.mean(resid_in * resid_in, -1, keepdims=True)) + EPS)
    attention_input = reduced_precision(resid_in * scale1 * gain_attn)
    q_proj = reduced_backward(matrix_multiply(attention_input, query_full)).reshape(span_length, QUERY_HEADS, HEAD_DIM)
    key_projected = reduced_backward(matrix_multiply(attention_input, complete_keys)).reshape(span_length, KEY_VALUE_HEADS, HEAD_DIM)
    value_vectors = reduced_backward(reduced_precision(matrix_multiply(attention_input, complete_values))).reshape(span_length, KEY_VALUE_HEADS, HEAD_DIM)
    gate_logit = reduced_backward(matrix_multiply(attention_input, headgate_full))
    q_scale = lax.rsqrt(lax.optimization_barrier(jnp.mean(q_proj * q_proj, -1, keepdims=True)) + EPS)
    k_scale = lax.rsqrt(lax.optimization_barrier(jnp.mean(key_projected * key_projected, -1, keepdims=True)) + EPS)
    q_normed = q_proj * q_scale * gain_query
    k_normed = key_projected * k_scale * gain_key
    query_rotated = reduced_precision(q_normed * cos_heads + rotate(q_normed) * sin_heads)
    k_rot = reduced_precision(k_normed * cos_heads + rotate(k_normed) * sin_heads)
    attn_val = reduced_backward(attention(query_rotated, k_rot, value_vectors, seg_row))
    gated = reduced_precision(attn_val * jax.nn.sigmoid(gate_logit)[:, :, None]).reshape(span_length, QUERY_HEADS * HEAD_DIM)
    hstate = resid_in + reduced_backward(matmul_t(gated, out_full))
    scale2 = lax.rsqrt(lax.optimization_barrier(jnp.mean(hstate * hstate, -1, keepdims=True)) + EPS)
    ffn_in = reduced_precision(hstate * scale2 * gain_ffn)
    gate_pre = reduced_backward(matrix_multiply(ffn_in, gate_full))
    up_pre = reduced_backward(matrix_multiply(ffn_in, up_full))
    hidden_act = reduced_precision(jax.nn.silu(gate_pre) * up_pre)
    return hstate + matmul_t(hidden_act, down_full)

def reference(tokens, segments, cotangent, norm_attn, w_query, key_matrix, value_matrix, w_headgate, query_gain, key_gain, w_out, norm_ffn, w_gate, w_up, w_down):
    params = tuple((weight.astype(jnp.float32) for weight in (norm_attn, w_query, key_matrix, value_matrix, w_headgate, query_gain, key_gain, w_out, norm_ffn, w_gate, w_up, w_down)))
    zeros_init = tuple((jnp.zeros_like(weight) for weight in params))

    def one_sequence(totals, seq_items):
        seq_tokens, seq_ids, seq_grad = seq_items

        def forward_fn(inputs, *weights):
            return block_forward(inputs, seq_ids, *weights)
        result, pull = jax.vjp(forward_fn, seq_tokens.astype(jnp.float32), *params)
        gradients = pull(seq_grad.astype(jnp.float32))
        new_totals = tuple((running + gradient for running, gradient in zip(totals, gradients[1:])))
        return (new_totals, (result.astype(jnp.bfloat16), gradients[0]))
    totals, (outputs, input_grads) = lax.scan(one_sequence, zeros_init, (tokens, segments, cotangent))
    return (outputs, input_grads, totals[0], totals[1], totals[2], totals[3], totals[4], totals[5], totals[6], totals[7], totals[8], totals[9], totals[10], totals[11])
```

```python
import math

import jax
import jax.numpy as jnp
from jax import lax
from jax.experimental import pallas as pl
from jax.experimental.pallas import tpu as pltpu
from jax.sharding import PartitionSpec as P

EPS = 1e-06
THETA = 1000000.0
DOC_MAX = 2048
LANES = 128
BF = jnp.bfloat16
F32 = jnp.float32
ANY = pl.BlockSpec(memory_space=pl.ANY)
ROWS = ("shard", "context")


def ring(x, axis, step):
    n = lax.axis_size(axis)
    return lax.ppermute(x, axis, [(i, (i + step) % n) for i in range(n)])


def line(x, axis, step):
    n = lax.axis_size(axis)
    return lax.ppermute(x, axis, [(i, i + step) for i in range(n) if 0 <= i + step < n])


def dot_t(a, b, ca, cb):
    return lax.dot_general(a, b, (((ca,), (cb,)), ((), ())), preferred_element_type=F32)


def place(pieces, index):
    count = len(pieces)
    rows, width = pieces[0].shape

    def body(idx, *refs):
        out, sems = refs[count], refs[count + 1]
        copies = [
            pltpu.make_async_copy(
                refs[j], out.at[pl.ds(pl.multiple_of(idx[j] * rows, rows), rows)], sems.at[j]
            )
            for j in range(count)
        ]
        for copy in copies:
            copy.start()
        for copy in copies:
            copy.wait()

    return pl.pallas_call(
        body,
        grid_spec=pltpu.PrefetchScalarGridSpec(
            num_scalar_prefetch=1,
            grid=(1,),
            in_specs=[ANY] * count,
            out_specs=pl.BlockSpec((count * rows, width), lambda i, idx: (0, 0)),
            scratch_shapes=[pltpu.SemaphoreType.DMA((count,))],
        ),
        out_shape=jax.ShapeDtypeStruct((count * rows, width), pieces[0].dtype),
        name="place",
    )(index, *pieces)


def gather_rows(weight):
    shards, chunks = lax.axis_size("shard"), lax.axis_size("context")
    s, c = lax.axis_index("shard"), lax.axis_index("context")
    mine = [weight] + [ring(weight, "context", k) for k in range(1, chunks)]
    pieces, index = list(mine), [s * chunks + (c - k) % chunks for k in range(chunks)]
    for t in range(1, shards):
        pieces += [ring(p, "shard", t) for p in mine]
        index += [((s - t) % shards) * chunks + (c - k) % chunks for k in range(chunks)]
    return place(pieces, jnp.stack(index).astype(jnp.int32))


def line_scatter(x):
    n, z = lax.axis_size("tensor"), lax.axis_index("tensor")
    rows = x.shape[0] // n

    def piece(i):
        return lax.dynamic_slice_in_dim(x, (i % n) * rows, rows, 0)

    right = left = None
    for step in range(n - 1):
        a, b = piece(z + n - 1 - step), piece(z + step - (n - 1))
        if step:
            a = (a.astype(F32) + right.astype(F32)).astype(BF)
            b = (b.astype(F32) + left.astype(F32)).astype(BF)
        right, left = line(a, "tensor", 1), line(b, "tensor", -1)
    return piece(z).astype(F32) + right.astype(F32) + left.astype(F32)


def line_gather(x):
    n, z = lax.axis_size("tensor"), lax.axis_index("tensor")
    rows, width = x.shape
    right, left, rights, lefts = x, x, [], []
    for _ in range(n - 1):
        right, left = line(right, "tensor", 1), line(left, "tensor", -1)
        rights.append(right)
        lefts.append(left)

    def body(zref, *refs):
        own, low, high = refs[0], refs[1:n], refs[n : 2 * n - 1]
        out, sems = refs[2 * n - 1], refs[2 * n]
        me = zref[0]

        def to(src, block, sem):
            return pltpu.make_async_copy(
                src, out.at[pl.ds(pl.multiple_of(block * rows, rows), rows)], sems.at[sem]
            )

        to(own, me, n - 1).start()
        for step in range(n - 1):
            block = lax.rem(me + (n - 1 - step), n)

            @pl.when(me > step)
            def _(step=step, block=block):
                to(low[step], block, step).start()

            @pl.when(me <= step)
            def _(step=step, block=block):
                to(high[n - 2 - step], block, step).start()

        for step in range(n):
            to(own, 0, step).wait()

    return pl.pallas_call(
        body,
        grid_spec=pltpu.PrefetchScalarGridSpec(
            num_scalar_prefetch=1,
            grid=(1,),
            in_specs=[ANY] * (2 * n - 1),
            out_specs=pl.BlockSpec((n * rows, width), lambda i, zref: (0, 0)),
            scratch_shapes=[pltpu.SemaphoreType.DMA((n,))],
        ),
        out_shape=jax.ShapeDtypeStruct((n * rows, width), x.dtype),
        name="join",
    )(z[None].astype(jnp.int32), x, *rights, *lefts)


def project_heads(qkv, cos_t, sin_t, gain_q, gain_k, q_heads, kv_heads):
    rows = qkv.shape[0]
    block = min(256, rows)
    kv_at, v_at = q_heads * LANES, (q_heads + kv_heads) * LANES

    def body(x_ref, c_ref, s_ref, gq_ref, gk_ref, q_ref, kv_ref):
        cos, sin = c_ref[...], s_ref[...]
        for h in range(q_heads + kv_heads):
            x = x_ref[:, h * LANES : (h + 1) * LANES]
            gain = gq_ref[...] if h < q_heads else gk_ref[...]
            v = x * lax.rsqrt(jnp.mean(x * x, -1, keepdims=True) + EPS) * gain
            v = (v * cos + pltpu.roll(v, LANES // 2, 1) * sin).astype(BF)
            if h < q_heads:
                q_ref[:, h * LANES : (h + 1) * LANES] = v
            else:
                g = h - q_heads
                kv_ref[:, g * LANES : (g + 1) * LANES] = v
        kv_ref[:, kv_heads * LANES :] = x_ref[:, v_at : v_at + kv_heads * LANES].astype(BF)

    def row(width):
        return pl.BlockSpec((block, width), lambda i: (i, 0))

    one = pl.BlockSpec((1, LANES), lambda i: (0, 0))
    return pl.pallas_call(
        body,
        grid=(rows // block,),
        in_specs=[row(qkv.shape[1]), row(LANES), row(LANES), one, one],
        out_specs=[row(kv_at), row(2 * kv_heads * LANES)],
        out_shape=[
            jax.ShapeDtypeStruct((rows, kv_at), BF),
            jax.ShapeDtypeStruct((rows, 2 * kv_heads * LANES), BF),
        ],
        name="project_heads",
    )(qkv, cos_t, sin_t, gain_q, gain_k)


def head_gate(misc, head):
    lane = lax.broadcasted_iota(jnp.int32, misc.shape, 1)
    return jax.nn.sigmoid(jnp.sum(jnp.where(lane == head, misc, 0.0), -1, keepdims=True))


def attend(q, window, qkv, start, q_heads, kv_heads):
    rows, keys = q.shape[0], window.shape[0]
    group = q_heads // kv_heads
    bq = bk = min(256, rows)
    count = rows // bq
    scale = math.log2(math.e) / math.sqrt(LANES)
    misc_at = qkv.shape[1] // LANES - 1

    def body(low, q_ref, k_ref, v_ref, m_ref, st_ref, o_ref, g_ref, l_ref):
        n, i = pl.program_id(0), pl.program_id(1)
        qs = jnp.concatenate([q_ref[:, h * LANES : (h + 1) * LANES] for h in range(group)], 0)
        st = jnp.concatenate([st_ref[...][:, :1]] * group, 0)
        at = keys - rows + i * bq + lax.broadcasted_iota(jnp.int32, (bq, 1), 0)
        at = jnp.concatenate([at] * group, 0)

        def step(j, carry):
            acc, total = carry
            base = pl.multiple_of(j * bk, bk)
            k, v = k_ref[pl.ds(base, bk), :], v_ref[pl.ds(base, bk), :]
            s = dot_t(qs, k, 1, 1) * scale
            col = base + lax.broadcasted_iota(jnp.int32, (1, bk), 1)
            p = jnp.where((col >= st) & (col <= at), jnp.exp2(s), 0.0)
            for b in range(bk // LANES):
                total = total + p[:, b * LANES : (b + 1) * LANES]
            return acc + dot_t(p.astype(BF), v, 1, 0), total

        zero = jnp.zeros((group * bq, LANES), F32)
        acc, total = lax.fori_loop(low[i], (keys - rows) // bk + i + 1, step, (zero, zero))
        total = jnp.sum(total, -1, keepdims=True)
        out = acc / total
        for h in range(group):
            o = out[h * bq : (h + 1) * bq]
            o_ref[:, h * LANES : (h + 1) * LANES] = o
            g_ref[:, h * LANES : (h + 1) * LANES] = (
                o * head_gate(m_ref[...], n * group + h)
            ).astype(BF)
        lse = jnp.broadcast_to(jnp.log2(total), (group * bq, LANES)).T
        l_ref[0, 0] = lse[:8]

    return pl.pallas_call(
        body,
        grid_spec=pltpu.PrefetchScalarGridSpec(
            num_scalar_prefetch=1,
            grid=(kv_heads, count),
            in_specs=[
                pl.BlockSpec((bq, group * LANES), lambda n, i, low: (i, n)),
                pl.BlockSpec((keys, LANES), lambda n, i, low: (0, n)),
                pl.BlockSpec((keys, LANES), lambda n, i, low: (0, kv_heads + n)),
                pl.BlockSpec((bq, LANES), lambda n, i, low: (i, misc_at)),
                pl.BlockSpec((bq, LANES), lambda n, i, low: (i, 0)),
            ],
            out_specs=[
                pl.BlockSpec((bq, group * LANES), lambda n, i, low: (i, n)),
                pl.BlockSpec((bq, group * LANES), lambda n, i, low: (i, n)),
                pl.BlockSpec((1, 1, 8, group * bq), lambda n, i, low: (n, i, 0, 0)),
            ],
        ),
        out_shape=[
            jax.ShapeDtypeStruct((rows, q_heads * LANES), F32),
            jax.ShapeDtypeStruct((rows, q_heads * LANES), BF),
            jax.ShapeDtypeStruct((kv_heads, count, 8, group * bq), F32),
        ],
        name="attend",
    )(start[::bq] // bk, q, window, window, qkv, jnp.broadcast_to(start[:, None], (rows, LANES)))


def attend_back(q, window, qkv, start, lse, grad_gated, attn_val, q_heads, kv_heads):
    rows, keys = q.shape[0], window.shape[0]
    group = q_heads // kv_heads
    bq = bk = min(256, rows)
    count = rows // bq
    root = 1.0 / math.sqrt(LANES)
    scale = math.log2(math.e) * root
    misc_at = qkv.shape[1] // LANES - 1

    def body(
        low, q_ref, k_ref, v_ref, m_ref, st_ref, l_ref, gg_ref, o_ref,
        dq_ref, dk_ref, dv_ref, gl_ref, dk_acc, dv_acc,
    ):
        n, i = pl.program_id(0), pl.program_id(1)

        @pl.when(i == 0)
        def _():
            dk_acc[...] = jnp.zeros_like(dk_acc)
            dv_acc[...] = jnp.zeros_like(dv_acc)

        qs = jnp.concatenate([q_ref[:, h * LANES : (h + 1) * LANES] for h in range(group)], 0)
        lane = lax.broadcasted_iota(jnp.int32, (bq, LANES), 1)
        logits, outs, centers = jnp.zeros((bq, LANES), F32), [], []
        for h in range(group):
            g, o = gg_ref[:, h * LANES : (h + 1) * LANES], o_ref[:, h * LANES : (h + 1) * LANES]
            sg = head_gate(m_ref[...], n * group + h)
            do = (g * sg).astype(BF)
            gl = jnp.sum(g * o, -1, keepdims=True) * sg * (1.0 - sg)
            logits = logits + jnp.where(lane == h, gl, 0.0)
            outs.append(do)
            centers.append(jnp.sum(do.astype(F32) * o, -1, keepdims=True))
        gl_ref[...] = logits
        dos = jnp.concatenate(outs, 0)
        center = jnp.broadcast_to(jnp.concatenate(centers, 0), (group * bq, LANES)).T[:1]
        top = l_ref[0, 0, :1]
        st = jnp.concatenate([st_ref[0, :1]] * group, 1)
        at = keys - rows + i * bq + lax.broadcasted_iota(jnp.int32, (1, bq), 1)
        at = jnp.concatenate([at] * group, 1)

        def step(j, dq):
            base = pl.multiple_of(j * bk, bk)
            part = pl.ds(base, bk)
            k, v = k_ref[part, :], v_ref[part, :]
            s = dot_t(k, qs, 1, 1) * scale
            pos = base + lax.broadcasted_iota(jnp.int32, (bk, 1), 0)
            p = jnp.where((pos >= st) & (pos <= at), jnp.exp2(s - top), 0.0)
            dp = dot_t(v, dos, 1, 1)
            ds = (p * (dp - center)).astype(BF)
            dv_acc[part, :] += dot_t(p.astype(BF), dos, 1, 0)
            dk_acc[part, :] += dot_t(ds, qs, 1, 0)
            return dq + dot_t(ds, k, 0, 0)

        dq = lax.fori_loop(
            low[i], (keys - rows) // bk + i + 1, step, jnp.zeros((group * bq, LANES), F32)
        )
        for h in range(group):
            dq_ref[:, h * LANES : (h + 1) * LANES] = dq[h * bq : (h + 1) * bq] * root

        @pl.when(i == count - 1)
        def _():
            dk_ref[...] = (dk_acc[...] * root).astype(BF)
            dv_ref[...] = dv_acc[...].astype(BF)

    wide = pl.BlockSpec((bq, group * LANES), lambda n, i, low: (i, n))
    key = pl.BlockSpec((keys, LANES), lambda n, i, low: (0, n))
    return pl.pallas_call(
        body,
        grid_spec=pltpu.PrefetchScalarGridSpec(
            num_scalar_prefetch=1,
            grid=(kv_heads, count),
            in_specs=[
                wide,
                key,
                pl.BlockSpec((keys, LANES), lambda n, i, low: (0, kv_heads + n)),
                pl.BlockSpec((bq, LANES), lambda n, i, low: (i, misc_at)),
                pl.BlockSpec((1, 8, bq), lambda n, i, low: (i, 0, 0)),
                pl.BlockSpec((1, 1, 8, group * bq), lambda n, i, low: (n, i, 0, 0)),
                wide,
                wide,
            ],
            out_specs=[wide, key, key, pl.BlockSpec((bq, LANES), lambda n, i, low: (i, n))],
            scratch_shapes=[pltpu.VMEM((keys, LANES), F32), pltpu.VMEM((keys, LANES), F32)],
        ),
        out_shape=[
            jax.ShapeDtypeStruct((rows, q_heads * LANES), F32),
            jax.ShapeDtypeStruct((keys, kv_heads * LANES), BF),
            jax.ShapeDtypeStruct((keys, kv_heads * LANES), BF),
            jax.ShapeDtypeStruct((rows, kv_heads * LANES), F32),
        ],
        name="attend_back",
    )(
        start[::bq] // bk,
        q,
        window,
        window,
        qkv,
        jnp.broadcast_to(start.reshape(count, 1, bq), (count, 8, bq)),
        lse,
        grad_gated,
        attn_val,
    )


def project_back(qkv, dq, dks, dvs, gl, cos_t, sin_t, gain_q, gain_k, q_heads, kv_heads):
    rows, width = qkv.shape
    block = min(256, rows)
    group = q_heads // kv_heads
    count = len(dks)

    def body(*refs):
        x_ref, dq_ref, gl_ref, c_ref, s_ref, gq_ref, gk_ref = refs[:7]
        dk_refs, dv_refs = refs[7 : 7 + count], refs[7 + count : 7 + 2 * count]
        out_ref, gain_ref = refs[7 + 2 * count :]

        @pl.when(pl.program_id(0) == 0)
        def _():
            gain_ref[...] = jnp.zeros_like(gain_ref)

        cos, sin = c_ref[...], s_ref[...]
        sums = [jnp.zeros((1, LANES), F32), jnp.zeros((1, LANES), F32)]
        for h in range(q_heads + kv_heads):
            x = x_ref[:, h * LANES : (h + 1) * LANES]
            if h < q_heads:
                g, gain, which = dq_ref[:, h * LANES : (h + 1) * LANES], gq_ref[...], 0
            else:
                part = slice((h - q_heads) * LANES, (h - q_heads + 1) * LANES)
                g = dk_refs[0][:, part].astype(F32)
                for ref in dk_refs[1:]:
                    g = g + ref[:, part].astype(F32)
                gain, which = gk_ref[...], 1
            g = g * cos - pltpu.roll(g, LANES // 2, 1) * sin
            r = lax.rsqrt(jnp.mean(x * x, -1, keepdims=True) + EPS)
            sums[which] = sums[which] + jnp.sum(g * x * r, 0, keepdims=True)
            gg = g * gain
            d = r * gg - x * (r * r * r * jnp.mean(gg * x, -1, keepdims=True))
            out_ref[:, h * LANES : (h + 1) * LANES] = d.astype(BF)
        first = (q_heads + kv_heads) * LANES
        dv = dv_refs[0][...].astype(F32)
        for ref in dv_refs[1:]:
            dv = dv + ref[...].astype(F32)
        out_ref[:, first : first + kv_heads * LANES] = dv.astype(BF)
        lane = lax.broadcasted_iota(jnp.int32, (block, LANES), 1)
        misc = jnp.zeros((block, LANES), F32)
        for h in range(q_heads):
            n, g = h // group, h % group
            col = gl_ref[:, n * LANES : (n + 1) * LANES][:, g : g + 1]
            misc = misc + jnp.where(lane == h, col, 0.0)
        out_ref[:, first + kv_heads * LANES :] = misc.astype(BF)
        gain_ref[...] += jnp.concatenate(sums + [jnp.zeros((6, LANES), F32)], 0)

    def row(w):
        return pl.BlockSpec((block, w), lambda i: (i, 0))

    one = pl.BlockSpec((1, LANES), lambda i: (0, 0))
    kv = row(kv_heads * LANES)
    return pl.pallas_call(
        body,
        grid=(rows // block,),
        in_specs=[row(width), row(q_heads * LANES), kv, row(LANES), row(LANES), one, one]
        + [kv] * (2 * count),
        out_specs=[row(width), pl.BlockSpec((8, LANES), lambda i: (0, 0))],
        out_shape=[
            jax.ShapeDtypeStruct((rows, width), BF),
            jax.ShapeDtypeStruct((8, LANES), F32),
        ],
        name="project_back",
    )(qkv, dq, gl, cos_t, sin_t, gain_q, gain_k, *dks, *dvs)


def per_device(
    tokens, segments, cotangent, norm_attn, w_query, key_matrix, value_matrix, w_headgate,
    query_gain, key_gain, w_out, norm_ffn, w_gate, w_up, w_down,
):
    chunks, shards = lax.axis_size("context"), lax.axis_size("shard")
    c, z = lax.axis_index("context"), lax.axis_index("tensor")
    _, rows, width = tokens.shape
    head = query_gain.shape[0] * shards * chunks
    q_heads, kv_heads = w_query.shape[1] // head, key_matrix.shape[1] // head
    q_cols, kv_cols = q_heads * head, kv_heads * head
    misc_at = q_cols + 2 * kv_cols
    share = rows // lax.axis_size("tensor")
    block_rows = norm_attn.shape[0]

    def column(v):
        return jnp.pad(v, (0, block_rows - v.shape[0]))[:, None]

    packed = jnp.concatenate(
        [
            w_query, key_matrix, value_matrix, w_headgate, column(norm_attn), column(norm_ffn),
            column(query_gain), column(key_gain),
            jnp.zeros((block_rows, LANES - q_heads - 4), BF),
        ],
        1,
    )
    pack = gather_rows(packed)
    gains = pack[:, misc_at + q_heads : misc_at + q_heads + 4].astype(F32).T
    gain_a, gain_f = gains[0], gains[1]
    head_gains = gains[2:].reshape(2, shards * chunks, block_rows)[:, :, : query_gain.shape[0]]
    gain_q, gain_k = head_gains[0].reshape(1, head), head_gains[1].reshape(1, head)

    reach = min(-(-(DOC_MAX - 1) // rows), chunks - 1)
    own_ids = segments[0]
    before = [
        jnp.where(c >= k, line(segments, "context", k)[0], -1) for k in range(reach, 0, -1)
    ]
    ids = jnp.concatenate(before + [own_ids])
    key_at = jnp.arange(ids.shape[0], dtype=jnp.int32)
    query_at = reach * rows + jnp.arange(rows, dtype=jnp.int32)
    place_in = jnp.sum(
        (ids[None, :] == own_ids[:, None]) & (key_at[None, :] < query_at[:, None]),
        axis=1,
        dtype=jnp.int32,
    )
    start = query_at - place_in
    frequency = jnp.exp(
        jnp.arange(head // 2, dtype=F32) * (-2.0 * math.log(THETA) / head)
    )
    angles = place_in.astype(F32)[:, None] * frequency
    cos_h, sin_h = jnp.cos(angles), jnp.sin(angles)
    cos_t = jnp.concatenate([cos_h, cos_h], -1)
    sin_t = jnp.concatenate([-sin_h, sin_h], -1)

    x = tokens[0].astype(F32)
    scale1 = lax.rsqrt(jnp.mean(x * x, -1, keepdims=True) + EPS)
    attn_in = (x * scale1 * gain_a).astype(BF)
    qkv = dot_t(attn_in, pack, 1, 0)
    q_rot, kv_rot = project_heads(qkv, cos_t, sin_t, gain_q, gain_k, q_heads, kv_heads)
    w_out, kv_rot = lax.optimization_barrier((w_out, kv_rot))
    window = jnp.concatenate(
        [line(kv_rot, "context", k) for k in range(reach, 0, -1)] + [kv_rot], 0
    )
    out_full = gather_rows(w_out)
    w_gate, w_up, w_down, window = lax.optimization_barrier((w_gate, w_up, w_down, window))
    gate_full, up_full, down_full = gather_rows(w_gate), gather_rows(w_up), gather_rows(w_down)

    attn_val, gated, lse = attend(q_rot, window, qkv, start, q_heads, kv_heads)
    attn_sum = line_scatter(dot_t(gated, out_full, 1, 1).astype(BF))

    own_x = lax.dynamic_slice_in_dim(tokens[0], z * share, share, 0).astype(F32)
    own_scale1 = lax.rsqrt(jnp.mean(own_x * own_x, -1, keepdims=True) + EPS)
    own_cot = lax.dynamic_slice_in_dim(cotangent[0], z * share, share, 0).astype(F32)
    hstate = own_x + attn_sum
    scale2 = lax.rsqrt(jnp.mean(hstate * hstate, -1, keepdims=True) + EPS)
    ffn_in = line_gather((hstate * scale2 * gain_f).astype(BF))

    gate_pre = dot_t(ffn_in, gate_full, 1, 0)
    up_pre = dot_t(ffn_in, up_full, 1, 0)
    gate_act = jax.nn.sigmoid(gate_pre)
    silu_act = gate_pre * gate_act
    hidden = (silu_act * up_pre).astype(BF)
    ffn_part = dot_t(hidden, down_full, 1, 1).astype(BF)
    cot = cotangent[0]
    grad_hid = dot_t(cot, down_full, 1, 0)
    grad_gp = (grad_hid * up_pre * gate_act * (1.0 + gate_pre * (1.0 - gate_act))).astype(BF)
    grad_up_pre = (grad_hid * silu_act).astype(BF)
    grad_ffn_part = (
        dot_t(grad_gp, gate_full, 1, 1) + dot_t(grad_up_pre, up_full, 1, 1)
    ).astype(BF)
    grad_ffn_in = line_scatter(grad_ffn_part)
    layer_own = (hstate + line_scatter(ffn_part)).astype(BF)
    layer_out = line_gather(layer_own)[None]

    grad_h = own_cot + scale2 * gain_f * grad_ffn_in - hstate * scale2**3 * jnp.mean(
        grad_ffn_in * gain_f * hstate, -1, keepdims=True
    )
    grad_h_low = line_gather(grad_h.astype(BF))
    grad_gated = dot_t(grad_h_low, out_full, 1, 0)

    def scattered(g):
        return lax.psum_scatter(g.astype(BF), ROWS, scatter_dimension=0, tiled=True).astype(F32)

    grad_down = scattered(dot_t(cot, hidden, 0, 0))
    grad_gate = scattered(dot_t(ffn_in, grad_gp, 0, 0))
    grad_up = scattered(dot_t(ffn_in, grad_up_pre, 0, 0))
    grad_out = scattered(dot_t(grad_h_low, gated, 0, 0))

    dq, dk, dv, gl = attend_back(
        q_rot, window, qkv, start, lse, grad_gated, attn_val, q_heads, kv_heads
    )

    def home(d):
        parts = [d[reach * rows :]]
        for k in range(1, reach + 1):
            parts.append(line(d[(reach - k) * rows : (reach - k + 1) * rows], "context", -k))
        return parts

    grad_pack, gain_sums = project_back(
        qkv, dq, home(dk), home(dv), gl, cos_t, sin_t, gain_q, gain_k, q_heads, kv_heads
    )
    grad_attn_in = line_scatter(dot_t(grad_pack, pack, 1, 1).astype(BF))
    def spread(v):
        v = v.reshape(shards * chunks, query_gain.shape[0])
        return jnp.pad(v, ((0, 0), (0, block_rows - v.shape[1]))).reshape(width, 1)

    lane = lax.broadcasted_iota(jnp.int32, (1, pack.shape[1]), 1) - misc_at - q_heads
    extra = jnp.where(lane == 2, spread(gain_sums[0]), 0.0) + jnp.where(
        lane == 3, spread(gain_sums[1]), 0.0
    )
    weight_grad = scattered(dot_t(attn_in, grad_pack, 0, 0) + extra)
    own_grad = grad_h + own_scale1 * gain_a * grad_attn_in - own_x * own_scale1**3 * jnp.mean(
        grad_attn_in * gain_a * own_x, -1, keepdims=True
    )
    tokens_grad = line_gather(own_grad.astype(BF)).astype(F32)[None]

    def weighted(w, g):
        return jnp.sum(w.astype(F32) * g, 1)

    used = misc_at + q_heads
    small = jnp.stack(
        [
            weighted(packed[:, :used], weight_grad[:, :used]) / norm_attn.astype(F32),
            (weighted(w_gate, grad_gate) + weighted(w_up, grad_up)) / norm_ffn.astype(F32),
            weight_grad[:, used + 2],
            weight_grad[:, used + 3],
        ]
    )
    small = sum([ring(small, "tensor", k) for k in range(1, lax.axis_size("tensor"))], small)

    return (
        layer_out,
        tokens_grad,
        small[0],
        weight_grad[:, :q_cols],
        weight_grad[:, q_cols : q_cols + kv_cols],
        weight_grad[:, q_cols + kv_cols : misc_at],
        weight_grad[:, misc_at : misc_at + q_heads],
        small[2, : query_gain.shape[0]],
        small[3, : query_gain.shape[0]],
        grad_out,
        small[1],
        grad_gate,
        grad_up,
        grad_down,
    )


def solution(mesh):
    row = P(("shard", "context"))
    weight = P(("shard", "context"), "tensor")
    act = P("shard", "context", None)
    in_specs = (
        act, P("shard", "context"), act, row, weight, weight, weight, weight, row, row, weight,
        row, weight, weight, weight,
    )
    out_specs = (
        act, act, row, weight, weight, weight, weight, row, row, weight, row, weight, weight,
        weight,
    )
    return jax.shard_map(
        per_device, mesh=mesh, in_specs=in_specs, out_specs=out_specs, check_vma=False
    )
```

```python
import math

import jax
import jax.numpy as jnp
from jax import lax
from jax.experimental import pallas as pl
from jax.experimental.pallas import tpu as pltpu
from jax.sharding import PartitionSpec as P

EPS = 1e-06
THETA = 1000000.0
DOC_MAX = 2048
LANES = 128
BF = jnp.bfloat16
F32 = jnp.float32
ANY = pl.BlockSpec(memory_space=pl.ANY)
ROWS = ("shard", "context")


def ring(x, axis, step):
    n = lax.axis_size(axis)
    return lax.ppermute(x, axis, [(i, (i + step) % n) for i in range(n)])


def line(x, axis, step):
    n = lax.axis_size(axis)
    return lax.ppermute(x, axis, [(i, i + step) for i in range(n) if 0 <= i + step < n])


def dot_t(a, b, ca, cb):
    return lax.dot_general(a, b, (((ca,), (cb,)), ((), ())), preferred_element_type=F32)


def place(pieces, rows_at, cols_at=None):
    count = len(pieces)
    cols_at = cols_at or [0] * count
    rows, width = pieces[0].shape
    wide = max(cols_at) + 1
    tall = count // wide

    def body(at, *refs):
        out, sems = refs[count], refs[count + 1]
        copies = [
            pltpu.make_async_copy(
                refs[j],
                out.at[
                    pl.ds(pl.multiple_of(at[j] * rows, rows), rows),
                    pl.ds(cols_at[j] * width, width),
                ],
                sems.at[j],
            )
            for j in range(count)
        ]
        for copy in copies:
            copy.start()
        for copy in copies:
            copy.wait()

    shape = (tall * rows, wide * width)
    return pl.pallas_call(
        body,
        grid_spec=pltpu.PrefetchScalarGridSpec(
            num_scalar_prefetch=1,
            grid=(1,),
            in_specs=[ANY] * count,
            out_specs=pl.BlockSpec(shape, lambda i, at: (0, 0)),
            scratch_shapes=[pltpu.SemaphoreType.DMA((count,))],
        ),
        out_shape=jax.ShapeDtypeStruct(shape, pieces[0].dtype),
        name="place",
    )(jnp.stack(rows_at).astype(jnp.int32), *pieces)


def gather_rows(weight):
    shards, chunks = lax.axis_size("shard"), lax.axis_size("context")
    s, c = lax.axis_index("shard"), lax.axis_index("context")
    mine = [weight] + [ring(weight, "context", k) for k in range(1, chunks)]
    pieces, index = list(mine), [s * chunks + (c - k) % chunks for k in range(chunks)]
    for t in range(1, shards):
        pieces += [ring(p, "shard", t) for p in mine]
        index += [((s - t) % shards) * chunks + (c - k) % chunks for k in range(chunks)]
    return place(pieces, index)


def gather_out(weight):
    shards, chunks = lax.axis_size("shard"), lax.axis_size("context")
    s, c = lax.axis_index("shard"), lax.axis_index("context")
    own = place(
        [weight] + [ring(weight, "context", k) for k in range(1, chunks)],
        [(c - k) % chunks for k in range(chunks)],
    )
    pieces, rows_at, cols_at = [], [], []
    for j, half in enumerate(ring_pieces(own)):
        for t in range(shards):
            pieces.append(half if t == 0 else ring(half, "shard", t))
            rows_at.append((s - t) % shards)
            cols_at.append(j)
    return place(pieces, rows_at, cols_at)


def ring_pieces(x):
    pieces = [x]
    for _ in range(lax.axis_size("tensor") - 1):
        pieces.append(ring(pieces[-1], "tensor", 1))
    return pieces


def ring_sum(pieces):
    got = None
    for piece in pieces[1:]:
        if got is not None:
            piece = (piece.astype(F32) + got.astype(F32)).astype(BF)
        got = ring(piece, "tensor", 1)
    return pieces[0].astype(F32) + (got.astype(F32) if got is not None else 0.0)


def blank(shape, dtype, name):
    return pl.pallas_call(
        lambda out: None, out_specs=ANY, out_shape=jax.ShapeDtypeStruct(shape, dtype), name=name
    )()


def lay_rows(pieces, dtype, name):
    n, z = lax.axis_size("tensor"), lax.axis_index("tensor")
    rows = pieces[0].shape[0]
    out = blank((n * rows, pieces[0].shape[1]), dtype, name)
    for j, piece in enumerate(pieces):
        out = lax.dynamic_update_slice_in_dim(out, piece.astype(dtype), ((z - j) % n) * rows, 0)
    return out


def project_heads(qkv, cos_t, sin_t, gain_q, gain_k, q_heads, kv_heads):
    rows = qkv.shape[0]
    block = min(256, rows)
    kv_at, v_at = q_heads * LANES, (q_heads + kv_heads) * LANES

    def body(x_ref, c_ref, s_ref, gq_ref, gk_ref, q_ref, kv_ref):
        cos, sin = c_ref[...], s_ref[...]
        for h in range(q_heads + kv_heads):
            x = x_ref[:, h * LANES : (h + 1) * LANES]
            gain = gq_ref[...] if h < q_heads else gk_ref[...]
            v = x * lax.rsqrt(jnp.mean(x * x, -1, keepdims=True) + EPS) * gain
            v = (v * cos + pltpu.roll(v, LANES // 2, 1) * sin).astype(BF)
            if h < q_heads:
                q_ref[:, h * LANES : (h + 1) * LANES] = v
            else:
                g = h - q_heads
                kv_ref[:, g * LANES : (g + 1) * LANES] = v
        kv_ref[:, kv_heads * LANES :] = x_ref[:, v_at : v_at + kv_heads * LANES].astype(BF)

    def row(width):
        return pl.BlockSpec((block, width), lambda i: (i, 0))

    one = pl.BlockSpec((1, LANES), lambda i: (0, 0))
    return pl.pallas_call(
        body,
        grid=(rows // block,),
        in_specs=[row(qkv.shape[1]), row(LANES), row(LANES), one, one],
        out_specs=[row(kv_at), row(2 * kv_heads * LANES)],
        out_shape=[
            jax.ShapeDtypeStruct((rows, kv_at), BF),
            jax.ShapeDtypeStruct((rows, 2 * kv_heads * LANES), BF),
        ],
        name="project_heads",
    )(qkv, cos_t, sin_t, gain_q, gain_k)


def head_gate(misc, head):
    lane = lax.broadcasted_iota(jnp.int32, misc.shape, 1)
    return jax.nn.sigmoid(jnp.sum(jnp.where(lane == head, misc, 0.0), -1, keepdims=True))


def attend(q, window, qkv, start, q_heads, kv_heads):
    rows, keys = q.shape[0], window.shape[0]
    group = q_heads // kv_heads
    bq = bk = min(256, rows)
    count = rows // bq
    scale = math.log2(math.e) / math.sqrt(LANES)
    misc_at = qkv.shape[1] // LANES - 1

    def body(low, q_ref, k_ref, v_ref, m_ref, st_ref, o_ref, g_ref, l_ref):
        n, i = pl.program_id(0), pl.program_id(1)
        qs = jnp.concatenate([q_ref[:, h * LANES : (h + 1) * LANES] for h in range(group)], 0)
        st = jnp.concatenate([st_ref[...][:, :1]] * group, 0)
        at = keys - rows + i * bq + lax.broadcasted_iota(jnp.int32, (bq, 1), 0)
        at = jnp.concatenate([at] * group, 0)

        def step(j, carry):
            acc, total = carry
            base = pl.multiple_of(j * bk, bk)
            k, v = k_ref[pl.ds(base, bk), :], v_ref[pl.ds(base, bk), :]
            s = dot_t(qs, k, 1, 1) * scale
            col = base + lax.broadcasted_iota(jnp.int32, (1, bk), 1)
            p = jnp.where((col >= st) & (col <= at), jnp.exp2(s), 0.0)
            for b in range(bk // LANES):
                total = total + p[:, b * LANES : (b + 1) * LANES]
            return acc + dot_t(p.astype(BF), v, 1, 0), total

        zero = jnp.zeros((group * bq, LANES), F32)
        acc, total = lax.fori_loop(low[i], (keys - rows) // bk + i + 1, step, (zero, zero))
        total = jnp.sum(total, -1, keepdims=True)
        out = acc / total
        for h in range(group):
            o = out[h * bq : (h + 1) * bq]
            o_ref[:, h * LANES : (h + 1) * LANES] = o
            g_ref[:, h * LANES : (h + 1) * LANES] = (
                o * head_gate(m_ref[...], n * group + h)
            ).astype(BF)
        lse = jnp.broadcast_to(jnp.log2(total), (group * bq, LANES)).T
        l_ref[0, 0] = lse[:8]

    return pl.pallas_call(
        body,
        grid_spec=pltpu.PrefetchScalarGridSpec(
            num_scalar_prefetch=1,
            grid=(kv_heads, count),
            in_specs=[
                pl.BlockSpec((bq, group * LANES), lambda n, i, low: (i, n)),
                pl.BlockSpec((keys, LANES), lambda n, i, low: (0, n)),
                pl.BlockSpec((keys, LANES), lambda n, i, low: (0, kv_heads + n)),
                pl.BlockSpec((bq, LANES), lambda n, i, low: (i, misc_at)),
                pl.BlockSpec((bq, LANES), lambda n, i, low: (i, 0)),
            ],
            out_specs=[
                pl.BlockSpec((bq, group * LANES), lambda n, i, low: (i, n)),
                pl.BlockSpec((bq, group * LANES), lambda n, i, low: (i, n)),
                pl.BlockSpec((1, 1, 8, group * bq), lambda n, i, low: (n, i, 0, 0)),
            ],
        ),
        out_shape=[
            jax.ShapeDtypeStruct((rows, q_heads * LANES), F32),
            jax.ShapeDtypeStruct((rows, q_heads * LANES), BF),
            jax.ShapeDtypeStruct((kv_heads, count, 8, group * bq), F32),
        ],
        name="attend",
    )(start[::bq] // bk, q, window, window, qkv, jnp.broadcast_to(start[:, None], (rows, LANES)))


def attend_back(q, window, qkv, start, lse, grad_gated, attn_val, q_heads, kv_heads):
    rows, keys = q.shape[0], window.shape[0]
    group = q_heads // kv_heads
    bq = bk = min(256, rows)
    count = rows // bq
    root = 1.0 / math.sqrt(LANES)
    scale = math.log2(math.e) * root
    misc_at = qkv.shape[1] // LANES - 1

    def body(
        low, q_ref, k_ref, v_ref, m_ref, st_ref, l_ref, gg_ref, o_ref,
        dq_ref, dk_ref, dv_ref, gl_ref, dk_acc, dv_acc,
    ):
        n, i = pl.program_id(0), pl.program_id(1)

        @pl.when(i == 0)
        def _():
            dk_acc[...] = jnp.zeros_like(dk_acc)
            dv_acc[...] = jnp.zeros_like(dv_acc)

        qs = jnp.concatenate([q_ref[:, h * LANES : (h + 1) * LANES] for h in range(group)], 0)
        lane = lax.broadcasted_iota(jnp.int32, (bq, LANES), 1)
        logits, outs, centers = jnp.zeros((bq, LANES), F32), [], []
        for h in range(group):
            g, o = gg_ref[:, h * LANES : (h + 1) * LANES], o_ref[:, h * LANES : (h + 1) * LANES]
            sg = head_gate(m_ref[...], n * group + h)
            do = (g * sg).astype(BF)
            gl = jnp.sum(g * o, -1, keepdims=True) * sg * (1.0 - sg)
            logits = logits + jnp.where(lane == h, gl, 0.0)
            outs.append(do)
            centers.append(jnp.sum(do.astype(F32) * o, -1, keepdims=True))
        gl_ref[...] = logits
        dos = jnp.concatenate(outs, 0)
        center = jnp.broadcast_to(jnp.concatenate(centers, 0), (group * bq, LANES)).T[:1]
        top = l_ref[0, 0, :1]
        st = jnp.concatenate([st_ref[0, :1]] * group, 1)
        at = keys - rows + i * bq + lax.broadcasted_iota(jnp.int32, (1, bq), 1)
        at = jnp.concatenate([at] * group, 1)

        def step(j, dq):
            base = pl.multiple_of(j * bk, bk)
            part = pl.ds(base, bk)
            k, v = k_ref[part, :], v_ref[part, :]
            s = dot_t(k, qs, 1, 1) * scale
            pos = base + lax.broadcasted_iota(jnp.int32, (bk, 1), 0)
            p = jnp.where((pos >= st) & (pos <= at), jnp.exp2(s - top), 0.0)
            dp = dot_t(v, dos, 1, 1)
            ds = (p * (dp - center)).astype(BF)
            dv_acc[part, :] += dot_t(p.astype(BF), dos, 1, 0)
            dk_acc[part, :] += dot_t(ds, qs, 1, 0)
            return dq + dot_t(ds, k, 0, 0)

        dq = lax.fori_loop(
            low[i], (keys - rows) // bk + i + 1, step, jnp.zeros((group * bq, LANES), F32)
        )
        for h in range(group):
            dq_ref[:, h * LANES : (h + 1) * LANES] = dq[h * bq : (h + 1) * bq] * root

        @pl.when(i == count - 1)
        def _():
            dk_ref[...] = (dk_acc[...] * root).astype(BF)
            dv_ref[...] = dv_acc[...].astype(BF)

    wide = pl.BlockSpec((bq, group * LANES), lambda n, i, low: (i, n))
    key = pl.BlockSpec((keys, LANES), lambda n, i, low: (0, n))
    return pl.pallas_call(
        body,
        grid_spec=pltpu.PrefetchScalarGridSpec(
            num_scalar_prefetch=1,
            grid=(kv_heads, count),
            in_specs=[
                wide,
                key,
                pl.BlockSpec((keys, LANES), lambda n, i, low: (0, kv_heads + n)),
                pl.BlockSpec((bq, LANES), lambda n, i, low: (i, misc_at)),
                pl.BlockSpec((1, 8, bq), lambda n, i, low: (i, 0, 0)),
                pl.BlockSpec((1, 1, 8, group * bq), lambda n, i, low: (n, i, 0, 0)),
                wide,
                wide,
            ],
            out_specs=[wide, key, key, pl.BlockSpec((bq, LANES), lambda n, i, low: (i, n))],
            scratch_shapes=[pltpu.VMEM((keys, LANES), F32), pltpu.VMEM((keys, LANES), F32)],
        ),
        out_shape=[
            jax.ShapeDtypeStruct((rows, q_heads * LANES), F32),
            jax.ShapeDtypeStruct((keys, kv_heads * LANES), BF),
            jax.ShapeDtypeStruct((keys, kv_heads * LANES), BF),
            jax.ShapeDtypeStruct((rows, kv_heads * LANES), F32),
        ],
        name="attend_back",
    )(
        start[::bq] // bk,
        q,
        window,
        window,
        qkv,
        jnp.broadcast_to(start.reshape(count, 1, bq), (count, 8, bq)),
        lse,
        grad_gated,
        attn_val,
    )


def project_back(qkv, dq, dks, dvs, gl, cos_t, sin_t, gain_q, gain_k, q_heads, kv_heads):
    rows, width = qkv.shape
    block = min(256, rows)
    group = q_heads // kv_heads
    count = len(dks)

    def body(*refs):
        x_ref, dq_ref, gl_ref, c_ref, s_ref, gq_ref, gk_ref = refs[:7]
        dk_refs, dv_refs = refs[7 : 7 + count], refs[7 + count : 7 + 2 * count]
        out_ref, gain_ref = refs[7 + 2 * count :]

        @pl.when(pl.program_id(0) == 0)
        def _():
            gain_ref[...] = jnp.zeros_like(gain_ref)

        cos, sin = c_ref[...], s_ref[...]
        sums = [jnp.zeros((1, LANES), F32), jnp.zeros((1, LANES), F32)]
        for h in range(q_heads + kv_heads):
            x = x_ref[:, h * LANES : (h + 1) * LANES]
            if h < q_heads:
                g, gain, which = dq_ref[:, h * LANES : (h + 1) * LANES], gq_ref[...], 0
            else:
                part = slice((h - q_heads) * LANES, (h - q_heads + 1) * LANES)
                g = dk_refs[0][:, part].astype(F32)
                for ref in dk_refs[1:]:
                    g = g + ref[:, part].astype(F32)
                gain, which = gk_ref[...], 1
            g = g * cos - pltpu.roll(g, LANES // 2, 1) * sin
            r = lax.rsqrt(jnp.mean(x * x, -1, keepdims=True) + EPS)
            sums[which] = sums[which] + jnp.sum(g * x * r, 0, keepdims=True)
            gg = g * gain
            d = r * gg - x * (r * r * r * jnp.mean(gg * x, -1, keepdims=True))
            out_ref[:, h * LANES : (h + 1) * LANES] = d.astype(BF)
        first = (q_heads + kv_heads) * LANES
        dv = dv_refs[0][...].astype(F32)
        for ref in dv_refs[1:]:
            dv = dv + ref[...].astype(F32)
        out_ref[:, first : first + kv_heads * LANES] = dv.astype(BF)
        lane = lax.broadcasted_iota(jnp.int32, (block, LANES), 1)
        misc = jnp.zeros((block, LANES), F32)
        for h in range(q_heads):
            n, g = h // group, h % group
            col = gl_ref[:, n * LANES : (n + 1) * LANES][:, g : g + 1]
            misc = misc + jnp.where(lane == h, col, 0.0)
        out_ref[:, first + kv_heads * LANES :] = misc.astype(BF)
        gain_ref[...] += jnp.concatenate(sums + [jnp.zeros((6, LANES), F32)], 0)

    def row(w):
        return pl.BlockSpec((block, w), lambda i: (i, 0))

    one = pl.BlockSpec((1, LANES), lambda i: (0, 0))
    kv = row(kv_heads * LANES)
    return pl.pallas_call(
        body,
        grid=(rows // block,),
        in_specs=[row(width), row(q_heads * LANES), kv, row(LANES), row(LANES), one, one]
        + [kv] * (2 * count),
        out_specs=[row(width), pl.BlockSpec((8, LANES), lambda i: (0, 0))],
        out_shape=[
            jax.ShapeDtypeStruct((rows, width), BF),
            jax.ShapeDtypeStruct((8, LANES), F32),
        ],
        name="project_back",
    )(qkv, dq, gl, cos_t, sin_t, gain_q, gain_k, *dks, *dvs)


def per_device(
    tokens, segments, cotangent, norm_attn, w_query, key_matrix, value_matrix, w_headgate,
    query_gain, key_gain, w_out, norm_ffn, w_gate, w_up, w_down,
):
    chunks, shards = lax.axis_size("context"), lax.axis_size("shard")
    c, z = lax.axis_index("context"), lax.axis_index("tensor")
    _, rows, width = tokens.shape
    head = query_gain.shape[0] * shards * chunks
    q_heads, kv_heads = w_query.shape[1] // head, key_matrix.shape[1] // head
    q_cols, kv_cols = q_heads * head, kv_heads * head
    misc_at = q_cols + 2 * kv_cols
    share = rows // lax.axis_size("tensor")
    block_rows = norm_attn.shape[0]

    def column(v):
        return jnp.pad(v, (0, block_rows - v.shape[0]))[:, None]

    packed = jnp.concatenate(
        [
            w_query, key_matrix, value_matrix, w_headgate, column(norm_attn), column(norm_ffn),
            column(query_gain), column(key_gain),
            jnp.zeros((block_rows, LANES - q_heads - 4), BF),
        ],
        1,
    )
    pack = gather_rows(packed)
    out_all = gather_out(w_out)
    gate_full, up_full, down_full = (
        lax.all_gather(w, ROWS, axis=0, tiled=True) for w in (w_gate, w_up, w_down)
    )
    gains = pack[:, misc_at + q_heads : misc_at + q_heads + 4].astype(F32).T
    gain_a, gain_f = gains[0], gains[1]
    head_gains = gains[2:].reshape(2, shards * chunks, block_rows)[:, :, : query_gain.shape[0]]
    gain_q, gain_k = head_gains[0].reshape(1, head), head_gains[1].reshape(1, head)

    reach = min(-(-(DOC_MAX - 1) // rows), chunks - 1)
    own_ids = segments[0]
    before = [
        jnp.where(c >= k, line(segments, "context", k)[0], -1) for k in range(reach, 0, -1)
    ]
    ids = jnp.concatenate(before + [own_ids])
    key_at = jnp.arange(ids.shape[0], dtype=jnp.int32)
    query_at = reach * rows + jnp.arange(rows, dtype=jnp.int32)
    place_in = jnp.sum(
        (ids[None, :] == own_ids[:, None]) & (key_at[None, :] < query_at[:, None]),
        axis=1,
        dtype=jnp.int32,
    )
    start = query_at - place_in
    frequency = jnp.exp(
        jnp.arange(head // 2, dtype=F32) * (-2.0 * math.log(THETA) / head)
    )
    angles = place_in.astype(F32)[:, None] * frequency
    cos_h, sin_h = jnp.cos(angles), jnp.sin(angles)
    cos_t = jnp.concatenate([cos_h, cos_h], -1)
    sin_t = jnp.concatenate([-sin_h, sin_h], -1)

    x = tokens[0].astype(F32)
    scale1 = lax.rsqrt(jnp.mean(x * x, -1, keepdims=True) + EPS)
    attn_in = (x * scale1 * gain_a).astype(BF)
    qkv = dot_t(attn_in, pack, 1, 0)
    q_rot, kv_rot = project_heads(qkv, cos_t, sin_t, gain_q, gain_k, q_heads, kv_heads)
    window = jnp.concatenate(
        [line(kv_rot, "context", k) for k in range(reach, 0, -1)] + [kv_rot], 0
    )

    attn_val, gated, lse = attend(q_rot, window, qkv, start, q_heads, kv_heads)
    n_tensor = lax.axis_size("tensor")

    def rows_of(a, j, at=0, size=share):
        return lax.dynamic_slice_in_dim(a, ((z - j) % n_tensor) * share + at, size, 0)

    heads = [rows_of(gated, 0)] + [
        ring(rows_of(gated, n_tensor - j), "tensor", j) for j in range(1, n_tensor)
    ]
    attn_sum = dot_t(jnp.concatenate(heads, 1), out_all, 1, 1)

    own_x = rows_of(tokens[0], 0).astype(F32)
    own_scale1 = lax.rsqrt(jnp.mean(own_x * own_x, -1, keepdims=True) + EPS)
    own_cot = rows_of(cotangent[0], 0).astype(F32)
    hstate = own_x + attn_sum
    scale2 = lax.rsqrt(jnp.mean(hstate * hstate, -1, keepdims=True) + EPS)
    own_in = (hstate * scale2 * gain_f).astype(BF)

    parts = 2
    size = share // parts
    cots, ins, hiddens, gps, ups, backs = [], [], [], [], [], []
    for p in range(parts):
        cots.append(
            jnp.concatenate([rows_of(cotangent[0], j, p * size, size) for j in range(n_tensor)], 0)
        )
        ins.append(jnp.concatenate(ring_pieces(own_in[p * size : (p + 1) * size]), 0))
        gate_pre = dot_t(ins[p], gate_full, 1, 0)
        up_pre = dot_t(ins[p], up_full, 1, 0)
        gate_act = jax.nn.sigmoid(gate_pre)
        silu_act = gate_pre * gate_act
        hiddens.append((silu_act * up_pre).astype(BF))
        grad_hid = dot_t(cots[p], down_full, 1, 0)
        gps.append(
            (grad_hid * up_pre * gate_act * (1.0 + gate_pre * (1.0 - gate_act))).astype(BF)
        )
        ups.append((grad_hid * silu_act).astype(BF))
        backs.append(
            (dot_t(gps[p], gate_full, 1, 1) + dot_t(ups[p], up_full, 1, 1)).astype(BF)
        )

    def split(a, size):
        return [a[j * size : (j + 1) * size] for j in range(n_tensor)]

    grad_ffn_in = jnp.concatenate([ring_sum(split(b, size)) for b in backs], 0)
    grad_h = own_cot + scale2 * gain_f * grad_ffn_in - hstate * scale2**3 * jnp.mean(
        grad_ffn_in * gain_f * hstate, -1, keepdims=True
    )
    grad_h_low = lay_rows(ring_pieces(grad_h.astype(BF)), BF, "grad_h_rows")
    grad_gated = dot_t(grad_h_low, out_all[:, :q_cols], 1, 0)

    cots, ins, hiddens, gps, ups, _ = lax.optimization_barrier(
        (cots, ins, hiddens, gps, ups, backs)
    )
    hiddens, _ = lax.optimization_barrier((hiddens, grad_h))
    cot, ffn_in, hidden, grad_gp, grad_up_pre = (
        jnp.concatenate(a, 0) for a in (cots, ins, hiddens, gps, ups)
    )

    def scattered(g):
        return lax.psum_scatter(g.astype(BF), ROWS, scatter_dimension=0, tiled=True).astype(F32)

    grad_gate = scattered(dot_t(ffn_in, grad_gp, 0, 0))
    grad_up = scattered(dot_t(ffn_in, grad_up_pre, 0, 0))
    grad_down = scattered(dot_t(cot, hidden, 0, 0))
    held, grad_h_low = lax.optimization_barrier((hidden, grad_h_low))
    ffn_part = dot_t(held, down_full, 1, 1).astype(BF).reshape(parts, n_tensor, size, width)
    ffn_sum = ring_sum([ffn_part[:, j].reshape(share, width) for j in range(n_tensor)])
    layer_out = lay_rows(ring_pieces((hstate + ffn_sum).astype(BF)), BF, "out_rows")[None]
    grad_out = scattered(dot_t(grad_h_low, gated, 0, 0))

    dq, dk, dv, gl = attend_back(
        q_rot, window, qkv, start, lse, grad_gated, attn_val, q_heads, kv_heads
    )

    def home(d):
        parts = [d[reach * rows :]]
        for k in range(1, reach + 1):
            parts.append(line(d[(reach - k) * rows : (reach - k + 1) * rows], "context", -k))
        return parts

    grad_pack, gain_sums = project_back(
        qkv, dq, home(dk), home(dv), gl, cos_t, sin_t, gain_q, gain_k, q_heads, kv_heads
    )
    attn_back = dot_t(grad_pack, pack, 1, 1).astype(BF)
    grad_attn_in = ring_sum([rows_of(attn_back, j) for j in range(n_tensor)])
    def spread(v):
        v = v.reshape(shards * chunks, query_gain.shape[0])
        return jnp.pad(v, ((0, 0), (0, block_rows - v.shape[1]))).reshape(width, 1)

    lane = lax.broadcasted_iota(jnp.int32, (1, pack.shape[1]), 1) - misc_at - q_heads
    extra = jnp.where(lane == 2, spread(gain_sums[0]), 0.0) + jnp.where(
        lane == 3, spread(gain_sums[1]), 0.0
    )
    weight_grad = scattered(dot_t(attn_in, grad_pack, 0, 0) + extra)
    own_grad = grad_h + own_scale1 * gain_a * grad_attn_in - own_x * own_scale1**3 * jnp.mean(
        grad_attn_in * gain_a * own_x, -1, keepdims=True
    )
    tokens_grad = lay_rows(ring_pieces(own_grad.astype(BF)), F32, "grad_rows")[None]

    def weighted(w, g):
        return jnp.sum(w.astype(F32) * g, 1)

    used = misc_at + q_heads
    small = jnp.stack(
        [
            weighted(packed[:, :used], weight_grad[:, :used]) / norm_attn.astype(F32),
            (weighted(w_gate, grad_gate) + weighted(w_up, grad_up)) / norm_ffn.astype(F32),
            weight_grad[:, used + 2],
            weight_grad[:, used + 3],
        ]
    )
    small = sum([ring(small, "tensor", k) for k in range(1, lax.axis_size("tensor"))], small)

    return (
        layer_out,
        tokens_grad,
        small[0],
        weight_grad[:, :q_cols],
        weight_grad[:, q_cols : q_cols + kv_cols],
        weight_grad[:, q_cols + kv_cols : misc_at],
        weight_grad[:, misc_at : misc_at + q_heads],
        small[2, : query_gain.shape[0]],
        small[3, : query_gain.shape[0]],
        grad_out,
        small[1],
        grad_gate,
        grad_up,
        grad_down,
    )


def solution(mesh):
    row = P(("shard", "context"))
    weight = P(("shard", "context"), "tensor")
    act = P("shard", "context", None)
    in_specs = (
        act, P("shard", "context"), act, row, weight, weight, weight, weight, row, row, weight,
        row, weight, weight, weight,
    )
    out_specs = (
        act, act, row, weight, weight, weight, weight, row, row, weight, row, weight, weight,
        weight,
    )
    return jax.shard_map(
        per_device, mesh=mesh, in_specs=in_specs, out_specs=out_specs, check_vma=False
    )
```

```python
import math

import jax
import jax.numpy as jnp
from jax import lax
from jax.experimental import pallas as pl
from jax.experimental.pallas import tpu as pltpu
from jax.sharding import PartitionSpec as P


EPS = 1e-06
THETA = 1000000.0
DOC_MAX = 2048
LANES = 128
BF = jnp.bfloat16
F32 = jnp.float32
ANY = pl.BlockSpec(memory_space=pl.ANY)
ROWS = ("shard", "context")


def ring(x, axis, step):
    n = lax.axis_size(axis)
    return lax.ppermute(x, axis, [(i, (i + step) % n) for i in range(n)])


def line(x, axis, step):
    n = lax.axis_size(axis)
    return lax.ppermute(x, axis, [(i, i + step) for i in range(n) if 0 <= i + step < n])


def tie(x, *first):
    return lax.optimization_barrier((x, first))[0]


def dot_t(a, b, ca, cb):
    return lax.dot_general(a, b, (((ca,), (cb,)), ((), ())), preferred_element_type=F32)


def place(pieces, rows_at, cols_at=None):
    count = len(pieces)
    cols_at = cols_at or [0] * count
    rows, width = pieces[0].shape
    wide = max(cols_at) + 1
    tall = count // wide

    def body(at, *refs):
        out, sems = refs[count], refs[count + 1]
        copies = [
            pltpu.make_async_copy(
                refs[j],
                out.at[
                    pl.ds(pl.multiple_of(at[j] * rows, rows), rows),
                    pl.ds(cols_at[j] * width, width),
                ],
                sems.at[j],
            )
            for j in range(count)
        ]
        for copy in copies:
            copy.start()
        for copy in copies:
            copy.wait()

    shape = (tall * rows, wide * width)
    return pl.pallas_call(
        body,
        grid_spec=pltpu.PrefetchScalarGridSpec(
            num_scalar_prefetch=1,
            grid=(1,),
            in_specs=[ANY] * count,
            out_specs=pl.BlockSpec(shape, lambda i, at: (0, 0)),
            scratch_shapes=[pltpu.SemaphoreType.DMA((count,))],
        ),
        out_shape=jax.ShapeDtypeStruct(shape, pieces[0].dtype),
        name="place",
    )(jnp.stack(rows_at).astype(jnp.int32), *pieces)


def gather_rows(weight):
    shards, chunks = lax.axis_size("shard"), lax.axis_size("context")
    s, c = lax.axis_index("shard"), lax.axis_index("context")
    mine = [weight] + [ring(weight, "context", k) for k in range(1, chunks)]
    pieces, index = list(mine), [s * chunks + (c - k) % chunks for k in range(chunks)]
    for t in range(1, shards):
        pieces += [ring(p, "shard", t) for p in mine]
        index += [((s - t) % shards) * chunks + (c - k) % chunks for k in range(chunks)]
    return place(pieces, index)


def gather_out(weight):
    chunks, c = lax.axis_size("context"), lax.axis_index("context")
    own = place(
        [weight] + [ring(weight, "context", k) for k in range(1, chunks)],
        [(c - k) % chunks for k in range(chunks)],
    )
    halves = [own]
    for j in range(1, lax.axis_size("tensor")):
        halves.append(ring(own, "tensor", j))
    return halves


def join_out(halves):
    shards, s = lax.axis_size("shard"), lax.axis_index("shard")
    pieces, rows_at, cols_at = [], [], []
    for j, half in enumerate(halves):
        for t in range(shards):
            pieces.append(half if t == 0 else ring(half, "shard", t))
            rows_at.append((s - t) % shards)
            cols_at.append(j)
    return place(pieces, rows_at, cols_at)


def ring_pieces(x):
    pieces = [x]
    for _ in range(lax.axis_size("tensor") - 1):
        pieces.append(ring(pieces[-1], "tensor", 1))
    return pieces


def ring_sum(pieces):
    got = None
    for piece in pieces[1:]:
        if got is not None:
            piece = (piece.astype(F32) + got.astype(F32)).astype(BF)
        got = ring(piece, "tensor", 1)
    return pieces[0].astype(F32) + got.astype(F32)


def scatter_rows(g):
    shards, chunks = lax.axis_size("shard"), lax.axis_size("context")
    s, c = lax.axis_index("shard"), lax.axis_index("context")

    def share(a, index, count, k):
        rows = a.shape[0] // count
        return lax.dynamic_slice_in_dim(a, ((index + k) % count) * rows, rows, 0)

    mid = share(g, s, shards, 0).astype(F32)
    for k in range(1, shards):
        mid = mid + ring(share(g, s, shards, k), "shard", k).astype(F32)
    mid = mid.astype(BF)
    total = share(mid, c, chunks, 0).astype(F32)
    for k in range(1, chunks):
        total = total + ring(share(mid, c, chunks, k), "context", k).astype(F32)
    return total


def blank(shape, dtype):
    return pl.pallas_call(
        lambda out: None, out_specs=ANY, out_shape=jax.ShapeDtypeStruct(shape, dtype)
    )()


def lay_rows(pieces, dtype):
    n, z = lax.axis_size("tensor"), lax.axis_index("tensor")
    rows = pieces[0].shape[0]
    out = blank((n * rows, pieces[0].shape[1]), dtype)
    for j, piece in enumerate(pieces):
        out = lax.dynamic_update_slice_in_dim(out, piece.astype(dtype), ((z - j) % n) * rows, 0)
    return out


def project_heads(qkv, cos_t, sin_t, gain_q, gain_k, q_heads, kv_heads):
    rows = qkv.shape[0]
    block = min(256, rows)
    kv_at, v_at = q_heads * LANES, (q_heads + kv_heads) * LANES

    def body(x_ref, c_ref, s_ref, gq_ref, gk_ref, q_ref, kv_ref):
        cos, sin = c_ref[...], s_ref[...]
        for h in range(q_heads + kv_heads):
            x = x_ref[:, h * LANES : (h + 1) * LANES]
            gain = gq_ref[...] if h < q_heads else gk_ref[...]
            v = x * lax.rsqrt(jnp.mean(x * x, -1, keepdims=True) + EPS) * gain
            v = (v * cos + pltpu.roll(v, LANES // 2, 1) * sin).astype(BF)
            if h < q_heads:
                q_ref[:, h * LANES : (h + 1) * LANES] = v
            else:
                g = h - q_heads
                kv_ref[:, g * LANES : (g + 1) * LANES] = v
        kv_ref[:, kv_heads * LANES :] = x_ref[:, v_at : v_at + kv_heads * LANES].astype(BF)

    def row(width):
        return pl.BlockSpec((block, width), lambda i: (i, 0))

    one = pl.BlockSpec((1, LANES), lambda i: (0, 0))
    return pl.pallas_call(
        body,
        grid=(rows // block,),
        in_specs=[row(qkv.shape[1]), row(LANES), row(LANES), one, one],
        out_specs=[row(kv_at), row(2 * kv_heads * LANES)],
        out_shape=[
            jax.ShapeDtypeStruct((rows, kv_at), BF),
            jax.ShapeDtypeStruct((rows, 2 * kv_heads * LANES), BF),
        ],
        name="project_heads",
    )(qkv, cos_t, sin_t, gain_q, gain_k)


def head_gate(misc, head):
    lane = lax.broadcasted_iota(jnp.int32, misc.shape, 1)
    return jax.nn.sigmoid(jnp.sum(jnp.where(lane == head, misc, 0.0), -1, keepdims=True))


def attend(q, window, qkv, start, q_heads, kv_heads):
    rows, keys = q.shape[0], window.shape[0]
    group = q_heads // kv_heads
    bq = bk = min(256, rows)
    count = rows // bq
    scale = math.log2(math.e) / math.sqrt(LANES)
    misc_at = qkv.shape[1] // LANES - 1

    def body(low, q_ref, k_ref, v_ref, m_ref, st_ref, o_ref, g_ref, l_ref):
        n, i = pl.program_id(0), pl.program_id(1)
        qs = jnp.concatenate([q_ref[:, h * LANES : (h + 1) * LANES] for h in range(group)], 0)
        st = jnp.concatenate([st_ref[...][:, :1]] * group, 0)
        at = keys - rows + i * bq + lax.broadcasted_iota(jnp.int32, (bq, 1), 0)
        at = jnp.concatenate([at] * group, 0)

        def step(j, carry):
            acc, total = carry
            base = pl.multiple_of(j * bk, bk)
            k, v = k_ref[pl.ds(base, bk), :], v_ref[pl.ds(base, bk), :]
            s = dot_t(qs, k, 1, 1) * scale
            col = base + lax.broadcasted_iota(jnp.int32, (1, bk), 1)
            p = jnp.where((col >= st) & (col <= at), jnp.exp2(s), 0.0)
            for b in range(bk // LANES):
                total = total + p[:, b * LANES : (b + 1) * LANES]
            return acc + dot_t(p.astype(BF), v, 1, 0), total

        zero = jnp.zeros((group * bq, LANES), F32)
        acc, total = lax.fori_loop(low[i], (keys - rows) // bk + i + 1, step, (zero, zero))
        total = jnp.sum(total, -1, keepdims=True)
        out = acc / total
        for h in range(group):
            o = out[h * bq : (h + 1) * bq]
            o_ref[:, h * LANES : (h + 1) * LANES] = o
            g_ref[:, h * LANES : (h + 1) * LANES] = (
                o * head_gate(m_ref[...], n * group + h)
            ).astype(BF)
        lse = jnp.broadcast_to(jnp.log2(total), (group * bq, LANES)).T
        l_ref[0, 0] = lse[:8]

    return pl.pallas_call(
        body,
        grid_spec=pltpu.PrefetchScalarGridSpec(
            num_scalar_prefetch=1,
            grid=(kv_heads, count),
            in_specs=[
                pl.BlockSpec((bq, group * LANES), lambda n, i, low: (i, n)),
                pl.BlockSpec((keys, LANES), lambda n, i, low: (0, n)),
                pl.BlockSpec((keys, LANES), lambda n, i, low: (0, kv_heads + n)),
                pl.BlockSpec((bq, LANES), lambda n, i, low: (i, misc_at)),
                pl.BlockSpec((bq, LANES), lambda n, i, low: (i, 0)),
            ],
            out_specs=[
                pl.BlockSpec((bq, group * LANES), lambda n, i, low: (i, n)),
                pl.BlockSpec((bq, group * LANES), lambda n, i, low: (i, n)),
                pl.BlockSpec((1, 1, 8, group * bq), lambda n, i, low: (n, i, 0, 0)),
            ],
        ),
        out_shape=[
            jax.ShapeDtypeStruct((rows, q_heads * LANES), F32),
            jax.ShapeDtypeStruct((rows, q_heads * LANES), BF),
            jax.ShapeDtypeStruct((kv_heads, count, 8, group * bq), F32),
        ],
        name="attend",
    )(start[::bq] // bk, q, window, window, qkv, jnp.broadcast_to(start[:, None], (rows, LANES)))


def attend_back(q, window, qkv, start, lse, grad_gated, attn_val, q_heads, kv_heads):
    rows, keys = q.shape[0], window.shape[0]
    group = q_heads // kv_heads
    bq = bk = min(256, rows)
    count = rows // bq
    root = 1.0 / math.sqrt(LANES)
    scale = math.log2(math.e) * root
    misc_at = qkv.shape[1] // LANES - 1

    def body(
        low, q_ref, k_ref, v_ref, m_ref, st_ref, l_ref, gg_ref, o_ref,
        dq_ref, dk_ref, dv_ref, gl_ref, dk_acc, dv_acc,
    ):
        n, i = pl.program_id(0), pl.program_id(1)

        @pl.when(i == 0)
        def _():
            dk_acc[...] = jnp.zeros_like(dk_acc)
            dv_acc[...] = jnp.zeros_like(dv_acc)

        qs = jnp.concatenate([q_ref[:, h * LANES : (h + 1) * LANES] for h in range(group)], 0)
        lane = lax.broadcasted_iota(jnp.int32, (bq, LANES), 1)
        logits, outs, centers = jnp.zeros((bq, LANES), F32), [], []
        for h in range(group):
            g, o = gg_ref[:, h * LANES : (h + 1) * LANES], o_ref[:, h * LANES : (h + 1) * LANES]
            sg = head_gate(m_ref[...], n * group + h)
            do = (g * sg).astype(BF)
            gl = jnp.sum(g * o, -1, keepdims=True) * sg * (1.0 - sg)
            logits = logits + jnp.where(lane == h, gl, 0.0)
            outs.append(do)
            centers.append(jnp.sum(do.astype(F32) * o, -1, keepdims=True))
        gl_ref[...] = logits
        dos = jnp.concatenate(outs, 0)
        center = jnp.broadcast_to(jnp.concatenate(centers, 0), (group * bq, LANES)).T[:1]
        top = l_ref[0, 0, :1]
        st = jnp.concatenate([st_ref[0, :1]] * group, 1)
        at = keys - rows + i * bq + lax.broadcasted_iota(jnp.int32, (1, bq), 1)
        at = jnp.concatenate([at] * group, 1)

        def step(j, dq):
            base = pl.multiple_of(j * bk, bk)
            part = pl.ds(base, bk)
            k, v = k_ref[part, :], v_ref[part, :]
            s = dot_t(k, qs, 1, 1) * scale
            pos = base + lax.broadcasted_iota(jnp.int32, (bk, 1), 0)
            p = jnp.where((pos >= st) & (pos <= at), jnp.exp2(s - top), 0.0)
            dp = dot_t(v, dos, 1, 1)
            ds = (p * (dp - center)).astype(BF)
            dv_acc[part, :] += dot_t(p.astype(BF), dos, 1, 0)
            dk_acc[part, :] += dot_t(ds, qs, 1, 0)
            return dq + dot_t(ds, k, 0, 0)

        dq = lax.fori_loop(
            low[i], (keys - rows) // bk + i + 1, step, jnp.zeros((group * bq, LANES), F32)
        )
        for h in range(group):
            dq_ref[:, h * LANES : (h + 1) * LANES] = dq[h * bq : (h + 1) * bq] * root

        @pl.when(i == count - 1)
        def _():
            dk_ref[...] = (dk_acc[...] * root).astype(BF)
            dv_ref[...] = dv_acc[...].astype(BF)

    wide = pl.BlockSpec((bq, group * LANES), lambda n, i, low: (i, n))
    key = pl.BlockSpec((keys, LANES), lambda n, i, low: (0, n))
    return pl.pallas_call(
        body,
        grid_spec=pltpu.PrefetchScalarGridSpec(
            num_scalar_prefetch=1,
            grid=(kv_heads, count),
            in_specs=[
                wide,
                key,
                pl.BlockSpec((keys, LANES), lambda n, i, low: (0, kv_heads + n)),
                pl.BlockSpec((bq, LANES), lambda n, i, low: (i, misc_at)),
                pl.BlockSpec((1, 8, bq), lambda n, i, low: (i, 0, 0)),
                pl.BlockSpec((1, 1, 8, group * bq), lambda n, i, low: (n, i, 0, 0)),
                wide,
                wide,
            ],
            out_specs=[wide, key, key, pl.BlockSpec((bq, LANES), lambda n, i, low: (i, n))],
            scratch_shapes=[pltpu.VMEM((keys, LANES), F32), pltpu.VMEM((keys, LANES), F32)],
        ),
        out_shape=[
            jax.ShapeDtypeStruct((rows, q_heads * LANES), F32),
            jax.ShapeDtypeStruct((keys, kv_heads * LANES), BF),
            jax.ShapeDtypeStruct((keys, kv_heads * LANES), BF),
            jax.ShapeDtypeStruct((rows, kv_heads * LANES), F32),
        ],
        name="attend_back",
    )(
        start[::bq] // bk,
        q,
        window,
        window,
        qkv,
        jnp.broadcast_to(start.reshape(count, 1, bq), (count, 8, bq)),
        lse,
        grad_gated,
        attn_val,
    )


def project_back(qkv, dq, dks, dvs, gl, cos_t, sin_t, gain_q, gain_k, q_heads, kv_heads):
    rows, width = qkv.shape
    block = min(256, rows)
    group = q_heads // kv_heads
    count = len(dks)

    def body(*refs):
        x_ref, dq_ref, gl_ref, c_ref, s_ref, gq_ref, gk_ref = refs[:7]
        dk_refs, dv_refs = refs[7 : 7 + count], refs[7 + count : 7 + 2 * count]
        out_ref, gain_ref = refs[7 + 2 * count :]

        @pl.when(pl.program_id(0) == 0)
        def _():
            gain_ref[...] = jnp.zeros_like(gain_ref)

        cos, sin = c_ref[...], s_ref[...]
        sums = [jnp.zeros((1, LANES), F32), jnp.zeros((1, LANES), F32)]
        for h in range(q_heads + kv_heads):
            x = x_ref[:, h * LANES : (h + 1) * LANES]
            if h < q_heads:
                g, gain, which = dq_ref[:, h * LANES : (h + 1) * LANES], gq_ref[...], 0
            else:
                part = slice((h - q_heads) * LANES, (h - q_heads + 1) * LANES)
                g = dk_refs[0][:, part].astype(F32)
                for ref in dk_refs[1:]:
                    g = g + ref[:, part].astype(F32)
                gain, which = gk_ref[...], 1
            g = g * cos - pltpu.roll(g, LANES // 2, 1) * sin
            r = lax.rsqrt(jnp.mean(x * x, -1, keepdims=True) + EPS)
            sums[which] = sums[which] + jnp.sum(g * x * r, 0, keepdims=True)
            gg = g * gain
            d = r * gg - x * (r * r * r * jnp.mean(gg * x, -1, keepdims=True))
            out_ref[:, h * LANES : (h + 1) * LANES] = d.astype(BF)
        first = (q_heads + kv_heads) * LANES
        dv = dv_refs[0][...].astype(F32)
        for ref in dv_refs[1:]:
            dv = dv + ref[...].astype(F32)
        out_ref[:, first : first + kv_heads * LANES] = dv.astype(BF)
        lane = lax.broadcasted_iota(jnp.int32, (block, LANES), 1)
        misc = jnp.zeros((block, LANES), F32)
        for h in range(q_heads):
            n, g = h // group, h % group
            col = gl_ref[:, n * LANES : (n + 1) * LANES][:, g : g + 1]
            misc = misc + jnp.where(lane == h, col, 0.0)
        out_ref[:, first + kv_heads * LANES :] = misc.astype(BF)
        gain_ref[...] += jnp.concatenate(sums + [jnp.zeros((6, LANES), F32)], 0)

    def row(w):
        return pl.BlockSpec((block, w), lambda i: (i, 0))

    one = pl.BlockSpec((1, LANES), lambda i: (0, 0))
    kv = row(kv_heads * LANES)
    return pl.pallas_call(
        body,
        grid=(rows // block,),
        in_specs=[row(width), row(q_heads * LANES), kv, row(LANES), row(LANES), one, one]
        + [kv] * (2 * count),
        out_specs=[row(width), pl.BlockSpec((8, LANES), lambda i: (0, 0))],
        out_shape=[
            jax.ShapeDtypeStruct((rows, width), BF),
            jax.ShapeDtypeStruct((8, LANES), F32),
        ],
        name="project_back",
    )(qkv, dq, gl, cos_t, sin_t, gain_q, gain_k, *dks, *dvs)


def per_device(
    tokens, segments, cotangent, norm_attn, w_query, key_matrix, value_matrix, w_headgate,
    query_gain, key_gain, w_out, norm_ffn, w_gate, w_up, w_down,
):
    chunks, shards = lax.axis_size("context"), lax.axis_size("shard")
    c, z = lax.axis_index("context"), lax.axis_index("tensor")
    _, rows, width = tokens.shape
    head = query_gain.shape[0] * shards * chunks
    q_heads, kv_heads = w_query.shape[1] // head, key_matrix.shape[1] // head
    q_cols, kv_cols = q_heads * head, kv_heads * head
    misc_at = q_cols + 2 * kv_cols
    share = rows // lax.axis_size("tensor")
    block_rows = norm_attn.shape[0]

    def column(v):
        return jnp.pad(v, (0, block_rows - v.shape[0]))[:, None]

    packed = jnp.concatenate(
        [
            w_query, key_matrix, value_matrix, w_headgate, column(norm_attn), column(norm_ffn),
            column(query_gain), column(key_gain),
            jnp.zeros((block_rows, LANES - q_heads - 4), BF),
        ],
        1,
    )
    pack = gather_rows(packed)
    out_halves = gather_out(tie(w_out, pack))
    gains = pack[:, misc_at + q_heads : misc_at + q_heads + 4].astype(F32).T
    gain_a, gain_f = gains[0], gains[1]
    head_gains = gains[2:].reshape(2, shards * chunks, block_rows)[:, :, : query_gain.shape[0]]
    gain_q, gain_k = head_gains[0].reshape(1, head), head_gains[1].reshape(1, head)

    reach = min(-(-(DOC_MAX - 1) // rows), chunks - 1)
    own_ids = segments[0]
    before = [
        jnp.where(c >= k, line(segments, "context", k)[0], -1) for k in range(reach, 0, -1)
    ]
    ids = jnp.concatenate(before + [own_ids])
    key_at = jnp.arange(ids.shape[0], dtype=jnp.int32)
    query_at = reach * rows + jnp.arange(rows, dtype=jnp.int32)
    place_in = jnp.sum(
        (ids[None, :] == own_ids[:, None]) & (key_at[None, :] < query_at[:, None]),
        axis=1,
        dtype=jnp.int32,
    )
    start = query_at - place_in
    frequency = jnp.exp(
        jnp.arange(head // 2, dtype=F32) * (-2.0 * math.log(THETA) / head)
    )
    angles = place_in.astype(F32)[:, None] * frequency
    cos_h, sin_h = jnp.cos(angles), jnp.sin(angles)
    cos_t = jnp.concatenate([cos_h, cos_h], -1)
    sin_t = jnp.concatenate([-sin_h, sin_h], -1)

    x = tokens[0].astype(F32)
    scale1 = lax.rsqrt(jnp.mean(x * x, -1, keepdims=True) + EPS)
    attn_in = (x * scale1 * gain_a).astype(BF)
    qkv = dot_t(attn_in, pack, 1, 0)
    q_rot, kv_rot = project_heads(qkv, cos_t, sin_t, gain_q, gain_k, q_heads, kv_heads)
    window = jnp.concatenate(
        [line(kv_rot, "context", k) for k in range(reach, 0, -1)] + [kv_rot], 0
    )

    def whole(w, *first):
        return lax.all_gather(tie(w, *first), ROWS, axis=0, tiled=True)

    gate_full = whole(w_gate, pack)
    up_full, down_full = whole(w_up, window), whole(w_down, window)

    attn_val, gated, lse = attend(q_rot, window, qkv, start, q_heads, kv_heads)
    n_tensor = lax.axis_size("tensor")

    def rows_of(a, j, at=0, size=share):
        return lax.dynamic_slice_in_dim(a, ((z - j) % n_tensor) * share + at, size, 0)

    heads = [rows_of(gated, 0)] + [
        ring(rows_of(gated, n_tensor - j), "tensor", j) for j in range(1, n_tensor)
    ]
    out_all = join_out(tie(out_halves, gated))
    attn_sum = dot_t(jnp.concatenate(heads, 1), out_all, 1, 1)

    own_x = rows_of(tokens[0], 0).astype(F32)
    own_scale1 = lax.rsqrt(jnp.mean(own_x * own_x, -1, keepdims=True) + EPS)
    own_cot = rows_of(cotangent[0], 0).astype(F32)
    hstate = own_x + attn_sum
    scale2 = lax.rsqrt(jnp.mean(hstate * hstate, -1, keepdims=True) + EPS)
    own_in = (hstate * scale2 * gain_f).astype(BF)

    parts = 2
    size = share // parts

    def split(a):
        return [a[j * size : (j + 1) * size] for j in range(n_tensor)]

    cots = [
        jnp.concatenate([rows_of(cotangent[0], j, p * size, size) for j in range(n_tensor)], 0)
        for p in range(parts)
    ]
    arriving = [ring_pieces(own_in[:size])]
    arriving.append(ring_pieces(tie(own_in[size:], arriving[0][-1])))
    ins, hiddens, gps, ups, sums = [], [], [], [], []
    for p in range(parts):
        ins.append(jnp.concatenate(arriving[p], 0))
        gate_pre = dot_t(ins[p], gate_full, 1, 0)
        up_pre = dot_t(ins[p], up_full, 1, 0)
        gate_act = jax.nn.sigmoid(gate_pre)
        silu_act = gate_pre * gate_act
        hiddens.append((silu_act * up_pre).astype(BF))
        grad_hid = dot_t(cots[p], down_full, 1, 0)
        gps.append((grad_hid * up_pre * gate_act * (1.0 + gate_pre * (1.0 - gate_act))).astype(BF))
        ups.append((grad_hid * silu_act).astype(BF))
        back = (dot_t(gps[p], gate_full, 1, 1) + dot_t(ups[p], up_full, 1, 1)).astype(BF)
        sums.append(ring_sum(split(back)))
    hiddens = tie(hiddens, back)
    ffn_parts = [dot_t(h, down_full, 1, 1).astype(BF) for h in hiddens]
    cot, hidden = jnp.concatenate(tie(cots, back), 0), jnp.concatenate(hiddens, 0)
    down_part = dot_t(cot, hidden, 0, 0).astype(BF)
    grad_ffn_in = jnp.concatenate(sums, 0)
    grad_h = own_cot + scale2 * gain_f * grad_ffn_in - hstate * scale2**3 * jnp.mean(
        grad_ffn_in * gain_f * hstate, -1, keepdims=True
    )
    own_low = grad_h.astype(BF)
    ffn_in, grad_gp = jnp.concatenate(tie(ins, back), 0), jnp.concatenate(tie(gps, back), 0)
    gate_part = dot_t(ffn_in, grad_gp, 0, 0).astype(BF)
    grad_up_pre = jnp.concatenate(tie(ups, back), 0)
    up_part = dot_t(ffn_in, grad_up_pre, 0, 0).astype(BF)
    low_pieces = ring_pieces(own_low)
    grad_h_low = lay_rows(low_pieces, BF)
    grad_gated = dot_t(grad_h_low, out_all[:, :q_cols], 1, 0)

    def scattered(g):
        return lax.psum_scatter(g, ROWS, scatter_dimension=0, tiled=True).astype(F32)

    grad_down, grad_gate = scattered(down_part), scattered(gate_part)

    ffn_pieces = [
        jnp.concatenate([f[j * size : (j + 1) * size] for f in ffn_parts], 0)
        for j in range(n_tensor)
    ]
    layer_own = hstate + ring_sum(tie(ffn_pieces, low_pieces[-1]))
    layer_out = lay_rows(ring_pieces(layer_own.astype(BF)), BF)[None]

    dq, dk, dv, gl = attend_back(
        q_rot, window, qkv, start, lse, grad_gated, attn_val, q_heads, kv_heads
    )
    out_part = dot_t(tie(grad_h_low, dq), gated, 0, 0).astype(BF)

    def home(d):
        parts = [d[reach * rows :]]
        for k in range(1, reach + 1):
            parts.append(line(d[(reach - k) * rows : (reach - k + 1) * rows], "context", -k))
        return parts

    dks, dvs = home(dk), home(dv)
    grad_up = scatter_rows(tie(up_part, dvs))
    grad_out = scatter_rows(out_part)
    grad_pack, gain_sums = project_back(
        qkv, dq, dks, dvs, gl, cos_t, sin_t, gain_q, gain_k, q_heads, kv_heads
    )
    attn_back = dot_t(grad_pack, pack, 1, 1).astype(BF)
    grad_attn_in = ring_sum([rows_of(attn_back, j) for j in range(n_tensor)])

    def spread(v):
        v = v.reshape(shards * chunks, query_gain.shape[0])
        return jnp.pad(v, ((0, 0), (0, block_rows - v.shape[1]))).reshape(width, 1)

    lane = lax.broadcasted_iota(jnp.int32, (1, pack.shape[1]), 1) - misc_at - q_heads
    extra = jnp.where(lane == 2, spread(gain_sums[0]), 0.0) + jnp.where(
        lane == 3, spread(gain_sums[1]), 0.0
    )
    pack_part = (dot_t(tie(attn_in, attn_back), grad_pack, 0, 0) + extra).astype(BF)
    weight_grad = scatter_rows(pack_part)
    own_grad = grad_h + own_scale1 * gain_a * grad_attn_in - own_x * own_scale1**3 * jnp.mean(
        grad_attn_in * gain_a * own_x, -1, keepdims=True
    )
    tokens_grad = lay_rows(ring_pieces(own_grad.astype(BF)), F32)[None]

    def weighted(w, g):
        return jnp.sum(w.astype(F32) * g, 1)

    used = misc_at + q_heads
    small = jnp.stack(
        [
            weighted(packed[:, :used], weight_grad[:, :used]) / norm_attn.astype(F32),
            (weighted(w_gate, grad_gate) + weighted(w_up, grad_up)) / norm_ffn.astype(F32),
            weight_grad[:, used + 2],
            weight_grad[:, used + 3],
        ]
    )
    small = sum([ring(small, "tensor", k) for k in range(1, lax.axis_size("tensor"))], small)

    return (
        layer_out,
        tokens_grad,
        small[0],
        weight_grad[:, :q_cols],
        weight_grad[:, q_cols : q_cols + kv_cols],
        weight_grad[:, q_cols + kv_cols : misc_at],
        weight_grad[:, misc_at : misc_at + q_heads],
        small[2, : query_gain.shape[0]],
        small[3, : query_gain.shape[0]],
        grad_out,
        small[1],
        grad_gate,
        grad_up,
        grad_down,
    )


def solution(mesh):
    row = P(("shard", "context"))
    weight = P(("shard", "context"), "tensor")
    act = P("shard", "context", None)
    in_specs = (
        act, P("shard", "context"), act, row, weight, weight, weight, weight, row, row, weight,
        row, weight, weight, weight,
    )
    out_specs = (
        act, act, row, weight, weight, weight, weight, row, row, weight, row, weight, weight,
        weight,
    )
    return jax.shard_map(
        per_device, mesh=mesh, in_specs=in_specs, out_specs=out_specs, check_vma=False
    )
```

```python
import math

import jax
import jax.numpy as jnp
from jax import lax
from jax.experimental import pallas as pl
from jax.experimental.pallas import tpu as pltpu
from jax.sharding import PartitionSpec as P


EPS = 1e-06
THETA = 1000000.0
DOC_MAX = 2048
LANES = 128
BF = jnp.bfloat16
F32 = jnp.float32
ANY = pl.BlockSpec(memory_space=pl.ANY)
SH, CT, TN = "shard", "context", "tensor"
ROWS = (SH, CT)


def ring(x, axis, step):
    n = lax.axis_size(axis)
    return lax.ppermute(x, axis, [(i, (i + step) % n) for i in range(n)])


def line(x, axis, step):
    n = lax.axis_size(axis)
    return lax.ppermute(x, axis, [(i, i + step) for i in range(n) if 0 <= i + step < n])


def tie(x, *first):
    return lax.optimization_barrier((x, first))[0]


def dot_t(a, b, ca, cb):
    return lax.dot_general(a, b, (((ca,), (cb,)), ((), ())), preferred_element_type=F32)


def place(pieces, rows_at, cols_at=None):
    count = len(pieces)
    cols_at = cols_at or [0] * count
    rows, width = pieces[0].shape
    wide = max(cols_at) + 1
    tall = count // wide

    def body(at, *refs):
        out, sems = refs[count], refs[count + 1]
        copies = [
            pltpu.make_async_copy(
                refs[j],
                out.at[
                    pl.ds(pl.multiple_of(at[j] * rows, rows), rows),
                    pl.ds(cols_at[j] * width, width),
                ],
                sems.at[j],
            )
            for j in range(count)
        ]
        for copy in copies:
            copy.start()
        for copy in copies:
            copy.wait()

    shape = (tall * rows, wide * width)
    return pl.pallas_call(
        body,
        grid_spec=pltpu.PrefetchScalarGridSpec(
            num_scalar_prefetch=1,
            grid=(1,),
            in_specs=[ANY] * count,
            out_specs=pl.BlockSpec(shape, lambda i, at: (0, 0)),
            scratch_shapes=[pltpu.SemaphoreType.DMA((count,))],
        ),
        out_shape=jax.ShapeDtypeStruct(shape, pieces[0].dtype),
        name="place",
    )(jnp.stack(rows_at).astype(jnp.int32), *pieces)


def row_pieces(weight):
    shards, chunks = lax.axis_size(SH), lax.axis_size(CT)
    s, c = lax.axis_index(SH), lax.axis_index(CT)
    mine = [weight] + [ring(weight, CT, k) for k in range(1, chunks)]
    pieces, index = list(mine), [s * chunks + (c - k) % chunks for k in range(chunks)]
    for t in range(1, shards):
        pieces += [ring(p, SH, t) for p in mine]
        index += [((s - t) % shards) * chunks + (c - k) % chunks for k in range(chunks)]
    return pieces, index


def gather_out(weight, first):
    chunks, c = lax.axis_size(CT), lax.axis_index(CT)
    pieces = [weight]
    for k in range(1, chunks):
        pieces.append(ring(weight, CT, k))
    own = place(tie(pieces, first), [(c - k) % chunks for k in range(chunks)])
    n = lax.axis_size(TN)
    halves = [own] + [None] * (n - 1)
    for j in range(1, n // 2 + 1):
        halves[j] = ring(halves[j - 1], TN, 1)
        if n - j > j:
            halves[n - j] = ring(halves[(n - j + 1) % n], TN, -1)
    return halves


def join_out(halves):
    shards, s = lax.axis_size(SH), lax.axis_index(SH)
    pieces, rows_at, cols_at = [], [], []
    for j, half in enumerate(halves):
        for t in range(shards):
            pieces.append(half if t == 0 else ring(half, SH, t))
            rows_at.append((s - t) % shards)
            cols_at.append(j)
    return place(pieces, rows_at, cols_at)


def ring_pieces(x, last_after=()):
    pieces, steps = [x], lax.axis_size(TN) - 1
    for k in range(steps):
        piece = tie(pieces[-1], last_after) if k == steps - 1 else pieces[-1]
        pieces.append(ring(piece, TN, 1))
    return pieces


def ring_sum(pieces):
    got = None
    for piece in pieces[1:]:
        if got is not None:
            piece = (piece.astype(F32) + got.astype(F32)).astype(BF)
        got = ring(piece, TN, 1)
    return pieces[0].astype(F32) + got.astype(F32)


def scatter_rows(g):
    shards, chunks = lax.axis_size(SH), lax.axis_size(CT)
    s, c = lax.axis_index(SH), lax.axis_index(CT)

    def share(a, index, count, k):
        rows = a.shape[0] // count
        return lax.dynamic_slice_in_dim(a, ((index + k) % count) * rows, rows, 0)

    mid = share(g, s, shards, 0).astype(F32)
    for k in range(1, shards):
        mid = mid + ring(share(g, s, shards, k), SH, k).astype(F32)
    mid = mid.astype(BF)
    total = share(mid, c, chunks, 0).astype(F32)
    for k in range(1, chunks):
        total = total + ring(share(mid, c, chunks, k), CT, k).astype(F32)
    return total


def blank(shape, dtype):
    return pl.pallas_call(
        lambda out: None, out_specs=ANY, out_shape=jax.ShapeDtypeStruct(shape, dtype)
    )()


def lay_rows(pieces, dtype):
    n, z = lax.axis_size(TN), lax.axis_index(TN)
    rows = pieces[0].shape[0]
    out = blank((n * rows, pieces[0].shape[1]), dtype)
    for j, piece in enumerate(pieces):
        out = lax.dynamic_update_slice_in_dim(out, piece.astype(dtype), ((z - j) % n) * rows, 0)
    return out


def project_heads(qkv, cos_t, sin_t, gain_q, gain_k, q_heads, kv_heads):
    rows = qkv.shape[0]
    block = min(256, rows)
    kv_at, v_at = q_heads * LANES, (q_heads + kv_heads) * LANES

    def body(x_ref, c_ref, s_ref, gq_ref, gk_ref, q_ref, kv_ref):
        cos, sin = c_ref[...], s_ref[...]
        for h in range(q_heads + kv_heads):
            x = x_ref[:, h * LANES : (h + 1) * LANES]
            gain = gq_ref[...] if h < q_heads else gk_ref[...]
            v = x * lax.rsqrt(jnp.mean(x * x, -1, keepdims=True) + EPS) * gain
            v = (v * cos + pltpu.roll(v, LANES // 2, 1) * sin).astype(BF)
            if h < q_heads:
                q_ref[:, h * LANES : (h + 1) * LANES] = v
            else:
                g = h - q_heads
                kv_ref[:, g * LANES : (g + 1) * LANES] = v
        kv_ref[:, kv_heads * LANES :] = x_ref[:, v_at : v_at + kv_heads * LANES].astype(BF)

    def row(width):
        return pl.BlockSpec((block, width), lambda i: (i, 0))

    one = pl.BlockSpec((1, LANES), lambda i: (0, 0))
    return pl.pallas_call(
        body,
        grid=(rows // block,),
        in_specs=[row(qkv.shape[1]), row(LANES), row(LANES), one, one],
        out_specs=[row(kv_at), row(2 * kv_heads * LANES)],
        out_shape=[
            jax.ShapeDtypeStruct((rows, kv_at), BF),
            jax.ShapeDtypeStruct((rows, 2 * kv_heads * LANES), BF),
        ],
        name="heads",
    )(qkv, cos_t, sin_t, gain_q, gain_k)


def head_gate(misc, head):
    lane = lax.broadcasted_iota(jnp.int32, misc.shape, 1)
    return jax.nn.sigmoid(jnp.sum(jnp.where(lane == head, misc, 0.0), -1, keepdims=True))


def attend(q, window, qkv, start, q_heads, kv_heads):
    rows, keys = q.shape[0], window.shape[0]
    group = q_heads // kv_heads
    bq = bk = min(256, rows)
    count = rows // bq
    scale = math.log2(math.e) / math.sqrt(LANES)
    misc_at = qkv.shape[1] // LANES - 1

    def body(low, q_ref, k_ref, v_ref, m_ref, st_ref, o_ref, g_ref, l_ref):
        n, i = pl.program_id(0), pl.program_id(1)
        qs = jnp.concatenate([q_ref[:, h * LANES : (h + 1) * LANES] for h in range(group)], 0)
        st = jnp.concatenate([st_ref[...][:, :1]] * group, 0)
        at = keys - rows + i * bq + lax.broadcasted_iota(jnp.int32, (bq, 1), 0)
        at = jnp.concatenate([at] * group, 0)

        def step(j, carry):
            acc, total = carry
            base = pl.multiple_of(j * bk, bk)
            k, v = k_ref[pl.ds(base, bk), :], v_ref[pl.ds(base, bk), :]
            s = dot_t(qs, k, 1, 1) * scale
            col = base + lax.broadcasted_iota(jnp.int32, (1, bk), 1)
            p = jnp.where((col >= st) & (col <= at), jnp.exp2(s), 0.0)
            for b in range(bk // LANES):
                total = total + p[:, b * LANES : (b + 1) * LANES]
            return acc + dot_t(p.astype(BF), v, 1, 0), total

        zero = jnp.zeros((group * bq, LANES), F32)
        acc, total = lax.fori_loop(low[i], (keys - rows) // bk + i + 1, step, (zero, zero))
        total = jnp.sum(total, -1, keepdims=True)
        out = acc / total
        for h in range(group):
            o = out[h * bq : (h + 1) * bq]
            o_ref[:, h * LANES : (h + 1) * LANES] = o
            g_ref[:, h * LANES : (h + 1) * LANES] = (
                o * head_gate(m_ref[...], n * group + h)
            ).astype(BF)
        lse = jnp.broadcast_to(jnp.log2(total), (group * bq, LANES)).T
        l_ref[0, 0] = lse[:8]

    return pl.pallas_call(
        body,
        grid_spec=pltpu.PrefetchScalarGridSpec(
            num_scalar_prefetch=1,
            grid=(kv_heads, count),
            in_specs=[
                pl.BlockSpec((bq, group * LANES), lambda n, i, low: (i, n)),
                pl.BlockSpec((keys, LANES), lambda n, i, low: (0, n)),
                pl.BlockSpec((keys, LANES), lambda n, i, low: (0, kv_heads + n)),
                pl.BlockSpec((bq, LANES), lambda n, i, low: (i, misc_at)),
                pl.BlockSpec((bq, LANES), lambda n, i, low: (i, 0)),
            ],
            out_specs=[
                pl.BlockSpec((bq, group * LANES), lambda n, i, low: (i, n)),
                pl.BlockSpec((bq, group * LANES), lambda n, i, low: (i, n)),
                pl.BlockSpec((1, 1, 8, group * bq), lambda n, i, low: (n, i, 0, 0)),
            ],
        ),
        out_shape=[
            jax.ShapeDtypeStruct((rows, q_heads * LANES), F32),
            jax.ShapeDtypeStruct((rows, q_heads * LANES), BF),
            jax.ShapeDtypeStruct((kv_heads, count, 8, group * bq), F32),
        ],
        name="attend",
    )(start[::bq] // bk, q, window, window, qkv, jnp.broadcast_to(start[:, None], (rows, LANES)))


def attend_back(q, window, qkv, start, lse, grad_gated, attn_val, q_heads, kv_heads):
    rows, keys = q.shape[0], window.shape[0]
    group = q_heads // kv_heads
    bq = bk = min(256, rows)
    count = rows // bq
    root = 1.0 / math.sqrt(LANES)
    scale = math.log2(math.e) * root
    misc_at = qkv.shape[1] // LANES - 1

    def body(
        low, q_ref, k_ref, v_ref, m_ref, st_ref, l_ref, gg_ref, o_ref,
        dq_ref, dk_ref, dv_ref, gl_ref, dk_acc, dv_acc,
    ):
        n, i = pl.program_id(0), pl.program_id(1)

        @pl.when(i == 0)
        def _():
            dk_acc[...] = jnp.zeros_like(dk_acc)
            dv_acc[...] = jnp.zeros_like(dv_acc)

        qs = jnp.concatenate([q_ref[:, h * LANES : (h + 1) * LANES] for h in range(group)], 0)
        lane = lax.broadcasted_iota(jnp.int32, (bq, LANES), 1)
        logits, outs, centers = jnp.zeros((bq, LANES), F32), [], []
        for h in range(group):
            g, o = gg_ref[:, h * LANES : (h + 1) * LANES].astype(F32), o_ref[:, h * LANES : (h + 1) * LANES]
            sg = head_gate(m_ref[...], n * group + h)
            do = (g * sg).astype(BF)
            gl = jnp.sum(g * o, -1, keepdims=True) * sg * (1.0 - sg)
            logits = logits + jnp.where(lane == h, gl, 0.0)
            outs.append(do)
            centers.append(jnp.sum(do.astype(F32) * o, -1, keepdims=True))
        gl_ref[...] = logits
        dos = jnp.concatenate(outs, 0)
        center = jnp.broadcast_to(jnp.concatenate(centers, 0), (group * bq, LANES)).T[:1]
        top = l_ref[0, 0, :1]
        st = jnp.concatenate([st_ref[0, :1]] * group, 1)
        at = keys - rows + i * bq + lax.broadcasted_iota(jnp.int32, (1, bq), 1)
        at = jnp.concatenate([at] * group, 1)

        def step(j, dq):
            base = pl.multiple_of(j * bk, bk)
            part = pl.ds(base, bk)
            k, v = k_ref[part, :], v_ref[part, :]
            s = dot_t(k, qs, 1, 1) * scale
            pos = base + lax.broadcasted_iota(jnp.int32, (bk, 1), 0)
            p = jnp.where((pos >= st) & (pos <= at), jnp.exp2(s - top), 0.0)
            dp = dot_t(v, dos, 1, 1)
            ds = (p * (dp - center)).astype(BF)
            dv_acc[part, :] += dot_t(p.astype(BF), dos, 1, 0)
            dk_acc[part, :] += dot_t(ds, qs, 1, 0)
            return dq + dot_t(ds, k, 0, 0)

        dq = lax.fori_loop(
            low[i], (keys - rows) // bk + i + 1, step, jnp.zeros((group * bq, LANES), F32)
        )
        for h in range(group):
            dq_ref[:, h * LANES : (h + 1) * LANES] = dq[h * bq : (h + 1) * bq] * root

        @pl.when(i == count - 1)
        def _():
            dk_ref[...] = (dk_acc[...] * root).astype(BF)
            dv_ref[...] = dv_acc[...].astype(BF)

    wide = pl.BlockSpec((bq, group * LANES), lambda n, i, low: (i, n))
    key = pl.BlockSpec((keys, LANES), lambda n, i, low: (0, n))
    return pl.pallas_call(
        body,
        grid_spec=pltpu.PrefetchScalarGridSpec(
            num_scalar_prefetch=1,
            grid=(kv_heads, count),
            in_specs=[
                wide,
                key,
                pl.BlockSpec((keys, LANES), lambda n, i, low: (0, kv_heads + n)),
                pl.BlockSpec((bq, LANES), lambda n, i, low: (i, misc_at)),
                pl.BlockSpec((1, 8, bq), lambda n, i, low: (i, 0, 0)),
                pl.BlockSpec((1, 1, 8, group * bq), lambda n, i, low: (n, i, 0, 0)),
                wide,
                wide,
            ],
            out_specs=[wide, key, key, pl.BlockSpec((bq, LANES), lambda n, i, low: (i, n))],
            scratch_shapes=[pltpu.VMEM((keys, LANES), F32), pltpu.VMEM((keys, LANES), F32)],
        ),
        out_shape=[
            jax.ShapeDtypeStruct((rows, q_heads * LANES), F32),
            jax.ShapeDtypeStruct((keys, kv_heads * LANES), BF),
            jax.ShapeDtypeStruct((keys, kv_heads * LANES), BF),
            jax.ShapeDtypeStruct((rows, kv_heads * LANES), F32),
        ],
        name="attend_back",
    )(
        start[::bq] // bk,
        q,
        window,
        window,
        qkv,
        jnp.broadcast_to(start.reshape(count, 1, bq), (count, 8, bq)),
        lse,
        grad_gated,
        attn_val,
    )


def project_back(qkv, dq, dks, dvs, gl, cos_t, sin_t, gain_q, gain_k, q_heads, kv_heads):
    rows, width = qkv.shape
    block = min(256, rows)
    group = q_heads // kv_heads
    count = len(dks)

    def body(*refs):
        x_ref, dq_ref, gl_ref, c_ref, s_ref, gq_ref, gk_ref = refs[:7]
        dk_refs, dv_refs = refs[7 : 7 + count], refs[7 + count : 7 + 2 * count]
        out_ref, gain_ref = refs[7 + 2 * count :]

        @pl.when(pl.program_id(0) == 0)
        def _():
            gain_ref[...] = jnp.zeros_like(gain_ref)

        cos, sin = c_ref[...], s_ref[...]
        sums = [jnp.zeros((1, LANES), F32), jnp.zeros((1, LANES), F32)]
        for h in range(q_heads + kv_heads):
            x = x_ref[:, h * LANES : (h + 1) * LANES]
            if h < q_heads:
                g, gain, which = dq_ref[:, h * LANES : (h + 1) * LANES], gq_ref[...], 0
            else:
                part = slice((h - q_heads) * LANES, (h - q_heads + 1) * LANES)
                g = dk_refs[0][:, part].astype(F32)
                for ref in dk_refs[1:]:
                    g = g + ref[:, part].astype(F32)
                gain, which = gk_ref[...], 1
            g = g * cos - pltpu.roll(g, LANES // 2, 1) * sin
            r = lax.rsqrt(jnp.mean(x * x, -1, keepdims=True) + EPS)
            sums[which] = sums[which] + jnp.sum(g * x * r, 0, keepdims=True)
            gg = g * gain
            d = r * gg - x * (r * r * r * jnp.mean(gg * x, -1, keepdims=True))
            out_ref[:, h * LANES : (h + 1) * LANES] = d.astype(BF)
        first = (q_heads + kv_heads) * LANES
        dv = dv_refs[0][...].astype(F32)
        for ref in dv_refs[1:]:
            dv = dv + ref[...].astype(F32)
        out_ref[:, first : first + kv_heads * LANES] = dv.astype(BF)
        lane = lax.broadcasted_iota(jnp.int32, (block, LANES), 1)
        misc = jnp.zeros((block, LANES), F32)
        for h in range(q_heads):
            n, g = h // group, h % group
            col = gl_ref[:, n * LANES : (n + 1) * LANES][:, g : g + 1]
            misc = misc + jnp.where(lane == h, col, 0.0)
        out_ref[:, first + kv_heads * LANES :] = misc.astype(BF)
        gain_ref[...] += jnp.concatenate(sums + [jnp.zeros((6, LANES), F32)], 0)

    def row(w):
        return pl.BlockSpec((block, w), lambda i: (i, 0))

    one = pl.BlockSpec((1, LANES), lambda i: (0, 0))
    kv = row(kv_heads * LANES)
    return pl.pallas_call(
        body,
        grid=(rows // block,),
        in_specs=[row(width), row(q_heads * LANES), kv, row(LANES), row(LANES), one, one]
        + [kv] * (2 * count),
        out_specs=[row(width), pl.BlockSpec((8, LANES), lambda i: (0, 0))],
        out_shape=[
            jax.ShapeDtypeStruct((rows, width), BF),
            jax.ShapeDtypeStruct((8, LANES), F32),
        ],
        name="heads_back",
    )(qkv, dq, gl, cos_t, sin_t, gain_q, gain_k, *dks, *dvs)


def per_device(
    tokens, segments, cotangent, norm_attn, w_query, key_matrix, value_matrix, w_headgate,
    query_gain, key_gain, w_out, norm_ffn, w_gate, w_up, w_down,
):
    chunks, shards = lax.axis_size(CT), lax.axis_size(SH)
    c, z = lax.axis_index(CT), lax.axis_index(TN)
    _, rows, width = tokens.shape
    head = query_gain.shape[0] * shards * chunks
    q_heads, kv_heads = w_query.shape[1] // head, key_matrix.shape[1] // head
    q_cols, kv_cols = q_heads * head, kv_heads * head
    misc_at = q_cols + 2 * kv_cols
    share = rows // lax.axis_size(TN)
    block_rows = norm_attn.shape[0]

    def column(v):
        return jnp.pad(v, (0, block_rows - v.shape[0]))[:, None]

    packed = jnp.concatenate(
        [
            w_query, key_matrix, value_matrix, w_headgate, column(norm_attn), column(norm_ffn),
            column(query_gain), column(key_gain),
            jnp.zeros((block_rows, LANES - q_heads - 4), BF),
        ],
        1,
    )
    pack_pieces, pack_index = row_pieces(packed)
    reach = min(-(-(DOC_MAX - 1) // rows), chunks - 1)
    own_ids = segments[0]
    earlier = [line(segments, CT, k)[0] for k in range(reach, 0, -1)]
    before = [jnp.where(c >= reach - i, e, -1) for i, e in enumerate(earlier)]
    ids = jnp.concatenate(before + [own_ids])
    key_at = jnp.arange(ids.shape[0], dtype=jnp.int32)
    query_at = reach * rows + jnp.arange(rows, dtype=jnp.int32)
    place_in = jnp.sum(
        (ids[None, :] == own_ids[:, None]) & (key_at[None, :] < query_at[:, None]),
        axis=1,
        dtype=jnp.int32,
    )
    start = query_at - place_in
    frequency = jnp.exp(
        jnp.arange(head // 2, dtype=F32) * (-2.0 * math.log(THETA) / head)
    )
    angles = place_in.astype(F32)[:, None] * frequency
    cos_h, sin_h = jnp.cos(angles), jnp.sin(angles)
    cos_t = jnp.concatenate([cos_h, cos_h], -1)
    sin_t = jnp.concatenate([-sin_h, sin_h], -1)

    x = tokens[0].astype(F32)
    scale1 = lax.rsqrt(jnp.mean(x * x, -1, keepdims=True) + EPS)

    pack = place(tie(pack_pieces, cos_t, sin_t, scale1), pack_index)
    out_halves = gather_out(tie(w_out, pack_pieces[:chunks]), pack)
    gains = pack[:, misc_at + q_heads : misc_at + q_heads + 4].astype(F32).T
    gain_a, gain_f = gains[0], gains[1]
    head_gains = gains[2:].reshape(2, shards * chunks, block_rows)[:, :, : query_gain.shape[0]]
    gain_q, gain_k = head_gains[0].reshape(1, head), head_gains[1].reshape(1, head)

    attn_in = (x * scale1 * gain_a).astype(BF)
    qkv = dot_t(attn_in, pack, 1, 0)
    q_rot, kv_rot = project_heads(qkv, cos_t, sin_t, gain_q, gain_k, q_heads, kv_heads)
    window = jnp.concatenate(
        [line(kv_rot, CT, k) for k in range(reach, 0, -1)] + [kv_rot], 0
    )

    def whole(w, *first):
        return lax.all_gather(tie(w, *first), ROWS, axis=0, tiled=True)

    gate_full = whole(w_gate, pack)
    up_full, down_full = whole(w_up, window), whole(w_down, window)

    attn_val, gated, lse = attend(
        tie(q_rot, gate_full), window, qkv, start, q_heads, kv_heads
    )
    n_tensor = lax.axis_size(TN)

    def rows_of(a, j, at=0, size=share):
        return lax.dynamic_slice_in_dim(a, ((z - j) % n_tensor) * share + at, size, 0)

    heads = [rows_of(gated, 0)]
    for j in range(1, n_tensor):
        heads.append(ring(rows_of(gated, n_tensor - j), TN, j))
    out_all = join_out(tie(out_halves, gated))
    own_gated = jnp.concatenate(heads, 1)
    attn_sum = dot_t(own_gated, out_all, 1, 1)

    own_x = rows_of(tokens[0], 0).astype(F32)
    own_scale1 = lax.rsqrt(jnp.mean(own_x * own_x, -1, keepdims=True) + EPS)
    own_cot = rows_of(cotangent[0], 0).astype(F32)
    hstate = own_x + attn_sum
    scale2 = lax.rsqrt(jnp.mean(hstate * hstate, -1, keepdims=True) + EPS)
    own_in = (hstate * scale2 * gain_f).astype(BF)

    parts = 2
    size = share // parts

    def split(a):
        return [a[j * size : (j + 1) * size] for j in range(n_tensor)]

    cots = [
        jnp.concatenate([rows_of(cotangent[0], j, p * size, size) for j in range(n_tensor)], 0)
        for p in range(parts)
    ]
    arriving = [ring_pieces(tie(own_in[:size], up_full))]
    arriving.append(ring_pieces(tie(own_in[size:], arriving[0][-1])))
    ins, hiddens, gps, ups, sums = [], [], [], [], []
    for p in range(parts):
        ins.append(jnp.concatenate(arriving[p], 0))
        gate_pre = dot_t(ins[p], gate_full, 1, 0)
        up_pre = dot_t(ins[p], up_full, 1, 0)
        gate_act = jax.nn.sigmoid(gate_pre)
        silu_act = gate_pre * gate_act
        hiddens.append((silu_act * up_pre).astype(BF))
        grad_hid = dot_t(cots[p], down_full, 1, 0)
        gps.append((grad_hid * up_pre * gate_act * (1.0 + gate_pre * (1.0 - gate_act))).astype(BF))
        ups.append((grad_hid * silu_act).astype(BF))
        back = (dot_t(gps[p], gate_full, 1, 1) + dot_t(ups[p], up_full, 1, 1)).astype(BF)
        sums.append(ring_sum(split(back)))
    hiddens = tie(hiddens, back)
    ffn_parts = [dot_t(h, down_full, 1, 1).astype(BF) for h in hiddens]
    cot, hidden = jnp.concatenate(tie(cots, back), 0), jnp.concatenate(hiddens, 0)
    down_part = dot_t(cot, hidden, 0, 0).astype(BF)
    grad_ffn_in = jnp.concatenate(sums, 0)
    grad_h = own_cot + scale2 * gain_f * grad_ffn_in - hstate * scale2**3 * jnp.mean(
        grad_ffn_in * gain_f * hstate, -1, keepdims=True
    )
    own_low = grad_h.astype(BF)
    ffn_in, grad_gp = jnp.concatenate(tie(ins, back), 0), jnp.concatenate(tie(gps, back), 0)
    gate_part = dot_t(ffn_in, grad_gp, 0, 0).astype(BF)
    grad_up_pre = jnp.concatenate(tie(ups, back), 0)
    up_part = dot_t(ffn_in, grad_up_pre, 0, 0).astype(BF)
    own_back = dot_t(own_low, out_all, 1, 0).astype(BF)
    back_rows, rows_at = [own_back[:, :q_cols]], [z]
    for j in range(1, n_tensor):
        back_rows.append(ring(own_back[:, j * q_cols : (j + 1) * q_cols], TN, -j))
        rows_at.append((z + j) % n_tensor)
    grad_gated = place(back_rows, rows_at)

    def scattered(g):
        return lax.psum_scatter(g, ROWS, scatter_dimension=0, tiled=True).astype(F32)

    grad_down = scatter_rows(down_part)
    grad_gate, grad_up = scattered(gate_part), scattered(up_part)

    ffn_pieces = [
        jnp.concatenate([f[j * size : (j + 1) * size] for f in ffn_parts], 0)
        for j in range(n_tensor)
    ]
    layer_own = hstate + ring_sum(tie(ffn_pieces, back_rows))
    layer_out = lay_rows(ring_pieces(layer_own.astype(BF)), BF)[None]

    dq, dk, dv, gl = attend_back(
        q_rot, window, qkv, start, lse, grad_gated, attn_val, q_heads, kv_heads
    )
    out_part = dot_t(tie(own_low, dq), own_gated, 0, 0).astype(BF)

    def home(d):
        parts = [d[reach * rows :]]
        for k in range(1, reach + 1):
            parts.append(line(d[(reach - k) * rows : (reach - k + 1) * rows], CT, -k))
        return parts

    dks, dvs = home(dk), home(dv)
    out_sum = scattered(out_part).astype(BF)
    grad_out = out_sum[:, :q_cols].astype(F32)
    for j in range(1, n_tensor):
        grad_out = grad_out + ring(out_sum[:, j * q_cols : (j + 1) * q_cols], TN, -j).astype(F32)
    grad_pack, gain_sums = project_back(
        qkv, tie(dq, grad_gate), dks, dvs, gl, cos_t, sin_t, gain_q, gain_k, q_heads, kv_heads
    )
    attn_back = dot_t(grad_pack, pack, 1, 1).astype(BF)
    grad_attn_in = ring_sum([rows_of(attn_back, j) for j in range(n_tensor)])
    grad_attn_in = tie(grad_attn_in, grad_up)

    def spread(v):
        v = v.reshape(shards * chunks, query_gain.shape[0])
        return jnp.pad(v, ((0, 0), (0, block_rows - v.shape[1]))).reshape(width, 1)

    lane = lax.broadcasted_iota(jnp.int32, (1, pack.shape[1]), 1) - misc_at - q_heads
    extra = jnp.where(lane == 2, spread(gain_sums[0]), 0.0) + jnp.where(
        lane == 3, spread(gain_sums[1]), 0.0
    )
    pack_part = (dot_t(tie(attn_in, attn_back), grad_pack, 0, 0) + extra).astype(BF)
    weight_grad = scattered(pack_part)
    own_grad = grad_h + own_scale1 * gain_a * grad_attn_in - own_x * own_scale1**3 * jnp.mean(
        grad_attn_in * gain_a * own_x, -1, keepdims=True
    )

    def weighted(w, g):
        return jnp.sum(w.astype(F32) * g, 1)

    used = misc_at + q_heads
    small = jnp.stack(
        [
            weighted(packed[:, :used], weight_grad[:, :used]) / norm_attn.astype(F32),
            (weighted(w_gate, grad_gate) + weighted(w_up, grad_up)) / norm_ffn.astype(F32),
            weight_grad[:, used + 2],
            weight_grad[:, used + 3],
        ]
    )
    small = sum([ring(small, TN, k) for k in range(1, n_tensor)], small)

    own_pieces = ring_pieces(own_grad.astype(BF))
    tokens_grad = lay_rows(own_pieces, F32)[None]

    return (
        layer_out,
        tokens_grad,
        small[0],
        weight_grad[:, :q_cols],
        weight_grad[:, q_cols : q_cols + kv_cols],
        weight_grad[:, q_cols + kv_cols : misc_at],
        weight_grad[:, misc_at : misc_at + q_heads],
        small[2, : query_gain.shape[0]],
        small[3, : query_gain.shape[0]],
        grad_out,
        small[1],
        grad_gate,
        grad_up,
        grad_down,
    )


def solution(mesh):
    row = P((SH, CT))
    weight = P((SH, CT), TN)
    act = P(SH, CT, None)
    in_specs = (
        act, P(SH, CT), act, row, weight, weight, weight, weight, row, row, weight,
        row, weight, weight, weight,
    )
    out_specs = (
        act, act, row, weight, weight, weight, weight, row, row, weight, row, weight, weight,
        weight,
    )
    return jax.shard_map(
        per_device, mesh=mesh, in_specs=in_specs, out_specs=out_specs, check_vma=False
    )
```

```python
import math

import jax
import jax.numpy as jnp
from jax import lax
from jax.experimental import pallas as pl
from jax.experimental.pallas import tpu as pltpu
from jax.sharding import PartitionSpec as P


EPS = 1e-06
THETA = 1000000.0
DOC_MAX = 2048
LANES = 128
BF = jnp.bfloat16
F32 = jnp.float32
ANY = pl.BlockSpec(memory_space=pl.ANY)
SH, CT, TN = "shard", "context", "tensor"
ROWS = (SH, CT)


def ring(x, axis, step):
    n = lax.axis_size(axis)
    return lax.ppermute(x, axis, [(i, (i + step) % n) for i in range(n)])


def line(x, axis, step):
    n = lax.axis_size(axis)
    return lax.ppermute(x, axis, [(i, i + step) for i in range(n) if 0 <= i + step < n])


def tie(x, *first):
    return lax.optimization_barrier((x, first))[0]


def dot_t(a, b, ca, cb):
    return lax.dot_general(a, b, (((ca,), (cb,)), ((), ())), preferred_element_type=F32)


def place(pieces, rows_at, cols_at=None):
    count = len(pieces)
    cols_at = cols_at or [0] * count
    rows, width = pieces[0].shape
    wide = max(cols_at) + 1
    tall = count // wide

    def body(at, *refs):
        out, sems = refs[count], refs[count + 1]
        copies = [
            pltpu.make_async_copy(
                refs[j],
                out.at[
                    pl.ds(pl.multiple_of(at[j] * rows, rows), rows),
                    pl.ds(cols_at[j] * width, width),
                ],
                sems.at[j],
            )
            for j in range(count)
        ]
        for copy in copies:
            copy.start()
        for copy in copies:
            copy.wait()

    shape = (tall * rows, wide * width)
    return pl.pallas_call(
        body,
        grid_spec=pltpu.PrefetchScalarGridSpec(
            num_scalar_prefetch=1,
            grid=(1,),
            in_specs=[ANY] * count,
            out_specs=pl.BlockSpec(shape, lambda i, at: (0, 0)),
            scratch_shapes=[pltpu.SemaphoreType.DMA((count,))],
        ),
        out_shape=jax.ShapeDtypeStruct(shape, pieces[0].dtype),
        name="place",
    )(jnp.stack(rows_at).astype(jnp.int32), *pieces)


def row_pieces(weight):
    shards, chunks = lax.axis_size(SH), lax.axis_size(CT)
    s, c = lax.axis_index(SH), lax.axis_index(CT)
    mine = [weight] + [ring(weight, CT, k) for k in range(1, chunks)]
    pieces, index = list(mine), [s * chunks + (c - k) % chunks for k in range(chunks)]
    for t in range(1, shards):
        pieces += [ring(p, SH, t) for p in mine]
        index += [((s - t) % shards) * chunks + (c - k) % chunks for k in range(chunks)]
    return pieces, index


def gather_out(weight, first):
    chunks, c = lax.axis_size(CT), lax.axis_index(CT)
    pieces = [weight]
    for k in range(1, chunks):
        pieces.append(ring(weight, CT, k))
    own = place(tie(pieces, first), [(c - k) % chunks for k in range(chunks)])
    n = lax.axis_size(TN)
    halves = [own] + [None] * (n - 1)
    for j in range(1, n // 2 + 1):
        halves[j] = ring(halves[j - 1], TN, 1)
        if n - j > j:
            halves[n - j] = ring(halves[(n - j + 1) % n], TN, -1)
    return halves


def join_out(halves):
    shards, s = lax.axis_size(SH), lax.axis_index(SH)
    pieces, rows_at, cols_at = [], [], []
    for j, half in enumerate(halves):
        for t in range(shards):
            pieces.append(half if t == 0 else ring(half, SH, t))
            rows_at.append((s - t) % shards)
            cols_at.append(j)
    return place(pieces, rows_at, cols_at)


def ring_pieces(x, last_after=()):
    pieces, steps = [x], lax.axis_size(TN) - 1
    for k in range(steps):
        piece = tie(pieces[-1], last_after) if k == steps - 1 else pieces[-1]
        pieces.append(ring(piece, TN, 1))
    return pieces


def ring_sum(pieces):
    got = None
    for piece in pieces[1:]:
        if got is not None:
            piece = (piece.astype(F32) + got.astype(F32)).astype(BF)
        got = ring(piece, TN, 1)
    return pieces[0].astype(F32) + got.astype(F32)


def scatter_rows(g):
    shards, chunks = lax.axis_size(SH), lax.axis_size(CT)
    s, c = lax.axis_index(SH), lax.axis_index(CT)

    def share(a, index, count, k):
        rows = a.shape[0] // count
        return lax.dynamic_slice_in_dim(a, ((index + k) % count) * rows, rows, 0)

    mid = share(g, s, shards, 0).astype(F32)
    for k in range(1, shards):
        mid = mid + ring(share(g, s, shards, k), SH, k).astype(F32)
    mid = mid.astype(BF)
    total = share(mid, c, chunks, 0).astype(F32)
    for k in range(1, chunks):
        total = total + ring(share(mid, c, chunks, k), CT, k).astype(F32)
    return total


def blank(shape, dtype):
    return pl.pallas_call(
        lambda out: None, out_specs=ANY, out_shape=jax.ShapeDtypeStruct(shape, dtype)
    )()


def lay_rows(pieces, dtype):
    n, z = lax.axis_size(TN), lax.axis_index(TN)
    rows = pieces[0].shape[0]
    out = blank((n * rows, pieces[0].shape[1]), dtype)
    for j, piece in enumerate(pieces):
        out = lax.dynamic_update_slice_in_dim(out, piece.astype(dtype), ((z - j) % n) * rows, 0)
    return out


def project_heads(qkv, cos_t, sin_t, gain_q, gain_k, q_heads, kv_heads):
    rows = qkv.shape[0]
    block = min(256, rows)
    kv_at, v_at = q_heads * LANES, (q_heads + kv_heads) * LANES

    def body(x_ref, c_ref, s_ref, gq_ref, gk_ref, q_ref, kv_ref):
        cos, sin = c_ref[...], s_ref[...]
        for h in range(q_heads + kv_heads):
            x = x_ref[:, h * LANES : (h + 1) * LANES]
            gain = gq_ref[...] if h < q_heads else gk_ref[...]
            v = x * lax.rsqrt(jnp.mean(x * x, -1, keepdims=True) + EPS) * gain
            v = (v * cos + pltpu.roll(v, LANES // 2, 1) * sin).astype(BF)
            if h < q_heads:
                q_ref[:, h * LANES : (h + 1) * LANES] = v
            else:
                g = h - q_heads
                kv_ref[:, g * LANES : (g + 1) * LANES] = v
        kv_ref[:, kv_heads * LANES :] = x_ref[:, v_at : v_at + kv_heads * LANES].astype(BF)

    def row(width):
        return pl.BlockSpec((block, width), lambda i: (i, 0))

    one = pl.BlockSpec((1, LANES), lambda i: (0, 0))
    return pl.pallas_call(
        body,
        grid=(rows // block,),
        in_specs=[row(qkv.shape[1]), row(LANES), row(LANES), one, one],
        out_specs=[row(kv_at), row(2 * kv_heads * LANES)],
        out_shape=[
            jax.ShapeDtypeStruct((rows, kv_at), BF),
            jax.ShapeDtypeStruct((rows, 2 * kv_heads * LANES), BF),
        ],
        name="heads",
    )(qkv, cos_t, sin_t, gain_q, gain_k)


def head_gate(misc, head):
    lane = lax.broadcasted_iota(jnp.int32, misc.shape, 1)
    return jax.nn.sigmoid(jnp.sum(jnp.where(lane == head, misc, 0.0), -1, keepdims=True))


def attend(q, window, qkv, start, q_heads, kv_heads):
    rows, keys = q.shape[0], window.shape[0]
    group = q_heads // kv_heads
    bq = min(256, rows)
    bk = min(2 * bq, rows)
    count = rows // bq
    scale = math.log2(math.e) / math.sqrt(LANES)
    misc_at = qkv.shape[1] // LANES - 1

    def body(low, q_ref, k_ref, v_ref, m_ref, st_ref, o_ref, g_ref, l_ref):
        n, i = pl.program_id(0), pl.program_id(1)
        qs = jnp.concatenate([q_ref[:, h * LANES : (h + 1) * LANES] for h in range(group)], 0)
        st = jnp.concatenate([st_ref[...][:, :1]] * group, 0)
        at = keys - rows + i * bq + lax.broadcasted_iota(jnp.int32, (bq, 1), 0)
        at = jnp.concatenate([at] * group, 0)

        def step(j, carry):
            acc, total = carry
            base = pl.multiple_of(j * bk, bk)
            k, v = k_ref[pl.ds(base, bk), :], v_ref[pl.ds(base, bk), :]
            s = dot_t(qs, k, 1, 1) * scale
            col = base + lax.broadcasted_iota(jnp.int32, (1, bk), 1)
            p = jnp.where((col >= st) & (col <= at), jnp.exp2(s), 0.0)
            for b in range(bk // LANES):
                total = total + p[:, b * LANES : (b + 1) * LANES]
            return acc + dot_t(p.astype(BF), v, 1, 0), total

        zero = jnp.zeros((group * bq, LANES), F32)
        acc, total = lax.fori_loop(low[i], (keys - rows + i * bq) // bk + 1, step, (zero, zero))
        total = jnp.sum(total, -1, keepdims=True)
        out = acc / total
        for h in range(group):
            o = out[h * bq : (h + 1) * bq]
            o_ref[:, h * LANES : (h + 1) * LANES] = o
            g_ref[:, h * LANES : (h + 1) * LANES] = (
                o * head_gate(m_ref[...], n * group + h)
            ).astype(BF)
        lse = jnp.broadcast_to(jnp.log2(total), (group * bq, LANES)).T
        l_ref[0, 0] = lse[:8]

    return pl.pallas_call(
        body,
        grid_spec=pltpu.PrefetchScalarGridSpec(
            num_scalar_prefetch=1,
            grid=(kv_heads, count),
            in_specs=[
                pl.BlockSpec((bq, group * LANES), lambda n, i, low: (i, n)),
                pl.BlockSpec((keys, LANES), lambda n, i, low: (0, n)),
                pl.BlockSpec((keys, LANES), lambda n, i, low: (0, kv_heads + n)),
                pl.BlockSpec((bq, LANES), lambda n, i, low: (i, misc_at)),
                pl.BlockSpec((bq, LANES), lambda n, i, low: (i, 0)),
            ],
            out_specs=[
                pl.BlockSpec((bq, group * LANES), lambda n, i, low: (i, n)),
                pl.BlockSpec((bq, group * LANES), lambda n, i, low: (i, n)),
                pl.BlockSpec((1, 1, 8, group * bq), lambda n, i, low: (n, i, 0, 0)),
            ],
        ),
        out_shape=[
            jax.ShapeDtypeStruct((rows, q_heads * LANES), F32),
            jax.ShapeDtypeStruct((rows, q_heads * LANES), BF),
            jax.ShapeDtypeStruct((kv_heads, count, 8, group * bq), F32),
        ],
        name="attend",
    )(start[::bq] // bk, q, window, window, qkv, jnp.broadcast_to(start[:, None], (rows, LANES)))


def attend_back(q, window, qkv, start, lse, grad_gated, attn_val, q_heads, kv_heads):
    rows, keys = q.shape[0], window.shape[0]
    group = q_heads // kv_heads
    bq = min(256, rows)
    bk = min(2 * bq, rows)
    count = rows // bq
    root = 1.0 / math.sqrt(LANES)
    scale = math.log2(math.e) * root
    misc_at = qkv.shape[1] // LANES - 1

    def body(
        low, q_ref, k_ref, v_ref, m_ref, st_ref, l_ref, gg_ref, o_ref,
        dq_ref, dk_ref, dv_ref, gl_ref, dk_acc, dv_acc,
    ):
        n, i = pl.program_id(0), pl.program_id(1)

        @pl.when(i == 0)
        def _():
            dk_acc[...] = jnp.zeros_like(dk_acc)
            dv_acc[...] = jnp.zeros_like(dv_acc)

        qs = jnp.concatenate([q_ref[:, h * LANES : (h + 1) * LANES] for h in range(group)], 0)
        lane = lax.broadcasted_iota(jnp.int32, (bq, LANES), 1)
        logits, outs, centers = jnp.zeros((bq, LANES), F32), [], []
        for h in range(group):
            g, o = gg_ref[:, h * LANES : (h + 1) * LANES].astype(F32), o_ref[:, h * LANES : (h + 1) * LANES]
            sg = head_gate(m_ref[...], n * group + h)
            do = (g * sg).astype(BF)
            gl = jnp.sum(g * o, -1, keepdims=True) * sg * (1.0 - sg)
            logits = logits + jnp.where(lane == h, gl, 0.0)
            outs.append(do)
            centers.append(jnp.sum(do.astype(F32) * o, -1, keepdims=True))
        gl_ref[...] = logits
        dos = jnp.concatenate(outs, 0)
        center = jnp.broadcast_to(jnp.concatenate(centers, 0), (group * bq, LANES)).T[:1]
        top = l_ref[0, 0, :1]
        st = jnp.concatenate([st_ref[0, :1]] * group, 1)
        at = keys - rows + i * bq + lax.broadcasted_iota(jnp.int32, (1, bq), 1)
        at = jnp.concatenate([at] * group, 1)

        def step(j, dq):
            base = pl.multiple_of(j * bk, bk)
            part = pl.ds(base, bk)
            k, v = k_ref[part, :], v_ref[part, :]
            s = dot_t(k, qs, 1, 1) * scale
            pos = base + lax.broadcasted_iota(jnp.int32, (bk, 1), 0)
            p = jnp.where((pos >= st) & (pos <= at), jnp.exp2(s - top), 0.0)
            dp = dot_t(v, dos, 1, 1)
            ds = (p * (dp - center)).astype(BF)
            dv_acc[part, :] += dot_t(p.astype(BF), dos, 1, 0)
            dk_acc[part, :] += dot_t(ds, qs, 1, 0)
            return dq + dot_t(ds, k, 0, 0)

        dq = lax.fori_loop(
            low[i],
            (keys - rows + i * bq) // bk + 1,
            step,
            jnp.zeros((group * bq, LANES), F32),
        )
        for h in range(group):
            dq_ref[:, h * LANES : (h + 1) * LANES] = dq[h * bq : (h + 1) * bq] * root

        @pl.when(i == count - 1)
        def _():
            dk_ref[...] = (dk_acc[...] * root).astype(BF)
            dv_ref[...] = dv_acc[...].astype(BF)

    wide = pl.BlockSpec((bq, group * LANES), lambda n, i, low: (i, n))
    key = pl.BlockSpec((keys, LANES), lambda n, i, low: (0, n))
    return pl.pallas_call(
        body,
        grid_spec=pltpu.PrefetchScalarGridSpec(
            num_scalar_prefetch=1,
            grid=(kv_heads, count),
            in_specs=[
                wide,
                key,
                pl.BlockSpec((keys, LANES), lambda n, i, low: (0, kv_heads + n)),
                pl.BlockSpec((bq, LANES), lambda n, i, low: (i, misc_at)),
                pl.BlockSpec((1, 8, bq), lambda n, i, low: (i, 0, 0)),
                pl.BlockSpec((1, 1, 8, group * bq), lambda n, i, low: (n, i, 0, 0)),
                wide,
                wide,
            ],
            out_specs=[wide, key, key, pl.BlockSpec((bq, LANES), lambda n, i, low: (i, n))],
            scratch_shapes=[pltpu.VMEM((keys, LANES), F32), pltpu.VMEM((keys, LANES), F32)],
        ),
        out_shape=[
            jax.ShapeDtypeStruct((rows, q_heads * LANES), F32),
            jax.ShapeDtypeStruct((keys, kv_heads * LANES), BF),
            jax.ShapeDtypeStruct((keys, kv_heads * LANES), BF),
            jax.ShapeDtypeStruct((rows, kv_heads * LANES), F32),
        ],
        name="attend_back",
    )(
        start[::bq] // bk,
        q,
        window,
        window,
        qkv,
        jnp.broadcast_to(start.reshape(count, 1, bq), (count, 8, bq)),
        lse,
        grad_gated,
        attn_val,
    )


def project_back(qkv, dq, dks, dvs, gl, cos_t, sin_t, gain_q, gain_k, q_heads, kv_heads):
    rows, width = qkv.shape
    block = min(256, rows)
    group = q_heads // kv_heads
    count = len(dks)

    def body(*refs):
        x_ref, dq_ref, gl_ref, c_ref, s_ref, gq_ref, gk_ref = refs[:7]
        dk_refs, dv_refs = refs[7 : 7 + count], refs[7 + count : 7 + 2 * count]
        out_ref, gain_ref = refs[7 + 2 * count :]

        @pl.when(pl.program_id(0) == 0)
        def _():
            gain_ref[...] = jnp.zeros_like(gain_ref)

        cos, sin = c_ref[...], s_ref[...]
        sums = [jnp.zeros((1, LANES), F32), jnp.zeros((1, LANES), F32)]
        for h in range(q_heads + kv_heads):
            x = x_ref[:, h * LANES : (h + 1) * LANES]
            if h < q_heads:
                g, gain, which = dq_ref[:, h * LANES : (h + 1) * LANES], gq_ref[...], 0
            else:
                part = slice((h - q_heads) * LANES, (h - q_heads + 1) * LANES)
                g = dk_refs[0][:, part].astype(F32)
                for ref in dk_refs[1:]:
                    g = g + ref[:, part].astype(F32)
                gain, which = gk_ref[...], 1
            g = g * cos - pltpu.roll(g, LANES // 2, 1) * sin
            r = lax.rsqrt(jnp.mean(x * x, -1, keepdims=True) + EPS)
            sums[which] = sums[which] + jnp.sum(g * x * r, 0, keepdims=True)
            gg = g * gain
            d = r * gg - x * (r * r * r * jnp.mean(gg * x, -1, keepdims=True))
            out_ref[:, h * LANES : (h + 1) * LANES] = d.astype(BF)
        first = (q_heads + kv_heads) * LANES
        dv = dv_refs[0][...].astype(F32)
        for ref in dv_refs[1:]:
            dv = dv + ref[...].astype(F32)
        out_ref[:, first : first + kv_heads * LANES] = dv.astype(BF)
        lane = lax.broadcasted_iota(jnp.int32, (block, LANES), 1)
        misc = jnp.zeros((block, LANES), F32)
        for h in range(q_heads):
            n, g = h // group, h % group
            col = gl_ref[:, n * LANES : (n + 1) * LANES][:, g : g + 1]
            misc = misc + jnp.where(lane == h, col, 0.0)
        out_ref[:, first + kv_heads * LANES :] = misc.astype(BF)
        gain_ref[...] += jnp.concatenate(sums + [jnp.zeros((6, LANES), F32)], 0)

    def row(w):
        return pl.BlockSpec((block, w), lambda i: (i, 0))

    one = pl.BlockSpec((1, LANES), lambda i: (0, 0))
    kv = row(kv_heads * LANES)
    return pl.pallas_call(
        body,
        grid=(rows // block,),
        in_specs=[row(width), row(q_heads * LANES), kv, row(LANES), row(LANES), one, one]
        + [kv] * (2 * count),
        out_specs=[row(width), pl.BlockSpec((8, LANES), lambda i: (0, 0))],
        out_shape=[
            jax.ShapeDtypeStruct((rows, width), BF),
            jax.ShapeDtypeStruct((8, LANES), F32),
        ],
        name="heads_back",
    )(qkv, dq, gl, cos_t, sin_t, gain_q, gain_k, *dks, *dvs)


def per_device(
    tokens, segments, cotangent, norm_attn, w_query, key_matrix, value_matrix, w_headgate,
    query_gain, key_gain, w_out, norm_ffn, w_gate, w_up, w_down,
):
    chunks, shards = lax.axis_size(CT), lax.axis_size(SH)
    c, z = lax.axis_index(CT), lax.axis_index(TN)
    _, rows, width = tokens.shape
    head = query_gain.shape[0] * shards * chunks
    q_heads, kv_heads = w_query.shape[1] // head, key_matrix.shape[1] // head
    q_cols, kv_cols = q_heads * head, kv_heads * head
    misc_at = q_cols + 2 * kv_cols
    share = rows // lax.axis_size(TN)
    block_rows = norm_attn.shape[0]

    def column(v):
        return jnp.pad(v, (0, block_rows - v.shape[0]))[:, None]

    packed = jnp.concatenate(
        [
            w_query, key_matrix, value_matrix, w_headgate, column(norm_attn), column(norm_ffn),
            column(query_gain), column(key_gain),
            jnp.zeros((block_rows, LANES - q_heads - 4), BF),
        ],
        1,
    )
    pack_pieces, pack_index = row_pieces(packed)
    reach = min(-(-(DOC_MAX - 1) // rows), chunks - 1)
    own_ids = segments[0]
    earlier = [line(segments, CT, k)[0] for k in range(reach, 0, -1)]
    before = [jnp.where(c >= reach - i, e, -1) for i, e in enumerate(earlier)]
    ids = jnp.concatenate(before + [own_ids])
    key_at = jnp.arange(ids.shape[0], dtype=jnp.int32)
    query_at = reach * rows + jnp.arange(rows, dtype=jnp.int32)
    place_in = jnp.sum(
        (ids[None, :] == own_ids[:, None]) & (key_at[None, :] < query_at[:, None]),
        axis=1,
        dtype=jnp.int32,
    )
    start = query_at - place_in
    frequency = jnp.exp(
        jnp.arange(head // 2, dtype=F32) * (-2.0 * math.log(THETA) / head)
    )
    angles = place_in.astype(F32)[:, None] * frequency
    cos_h, sin_h = jnp.cos(angles), jnp.sin(angles)
    cos_t = jnp.concatenate([cos_h, cos_h], -1)
    sin_t = jnp.concatenate([-sin_h, sin_h], -1)

    x = tokens[0].astype(F32)
    scale1 = lax.rsqrt(jnp.mean(x * x, -1, keepdims=True) + EPS)

    pack = place(tie(pack_pieces, cos_t, sin_t, scale1), pack_index)
    out_halves = gather_out(tie(w_out, pack_pieces[:chunks]), pack)
    gains = pack[:, misc_at + q_heads : misc_at + q_heads + 4].astype(F32).T
    gain_a, gain_f = gains[0], gains[1]
    head_gains = gains[2:].reshape(2, shards * chunks, block_rows)[:, :, : query_gain.shape[0]]
    gain_q, gain_k = head_gains[0].reshape(1, head), head_gains[1].reshape(1, head)

    attn_in = (x * scale1 * gain_a).astype(BF)
    qkv = dot_t(attn_in, pack, 1, 0)
    q_rot, kv_rot = project_heads(qkv, cos_t, sin_t, gain_q, gain_k, q_heads, kv_heads)
    window = jnp.concatenate(
        [line(kv_rot, CT, k) for k in range(reach, 0, -1)] + [kv_rot], 0
    )

    def whole(w, *first):
        return lax.all_gather(tie(w, *first), ROWS, axis=0, tiled=True)

    gate_full = whole(w_gate, pack)
    up_full, down_full = whole(w_up, window), whole(w_down, window)

    attn_val, gated, lse = attend(
        tie(q_rot, gate_full), window, qkv, start, q_heads, kv_heads
    )
    n_tensor = lax.axis_size(TN)

    def rows_of(a, j, at=0, size=share):
        return lax.dynamic_slice_in_dim(a, ((z - j) % n_tensor) * share + at, size, 0)

    heads = [rows_of(gated, 0)]
    for j in range(1, n_tensor):
        heads.append(ring(rows_of(gated, n_tensor - j), TN, j))
    out_all = join_out(tie(out_halves, gated))
    own_gated = jnp.concatenate(heads, 1)
    attn_sum = dot_t(own_gated, out_all, 1, 1)

    own_x = rows_of(tokens[0], 0).astype(F32)
    own_scale1 = lax.rsqrt(jnp.mean(own_x * own_x, -1, keepdims=True) + EPS)
    own_cot = rows_of(cotangent[0], 0).astype(F32)
    hstate = own_x + attn_sum
    scale2 = lax.rsqrt(jnp.mean(hstate * hstate, -1, keepdims=True) + EPS)
    own_in = (hstate * scale2 * gain_f).astype(BF)

    parts = 2
    size = share // parts

    def split(a):
        return [a[j * size : (j + 1) * size] for j in range(n_tensor)]

    cots = [
        jnp.concatenate([rows_of(cotangent[0], j, p * size, size) for j in range(n_tensor)], 0)
        for p in range(parts)
    ]
    arriving = [ring_pieces(tie(own_in[:size], up_full))]
    arriving.append(ring_pieces(tie(own_in[size:], arriving[0][-1])))
    ins, hiddens, gps, ups, sums = [], [], [], [], []
    for p in range(parts):
        ins.append(jnp.concatenate(arriving[p], 0))
        gate_pre = dot_t(ins[p], gate_full, 1, 0)
        up_pre = dot_t(ins[p], up_full, 1, 0)
        gate_act = jax.nn.sigmoid(gate_pre)
        silu_act = gate_pre * gate_act
        hiddens.append((silu_act * up_pre).astype(BF))
        grad_hid = dot_t(cots[p], down_full, 1, 0)
        gps.append((grad_hid * up_pre * gate_act * (1.0 + gate_pre * (1.0 - gate_act))).astype(BF))
        ups.append((grad_hid * silu_act).astype(BF))
        back = (dot_t(gps[p], gate_full, 1, 1) + dot_t(ups[p], up_full, 1, 1)).astype(BF)
        sums.append(ring_sum(split(back)))
    hiddens = tie(hiddens, back)
    ffn_parts = [dot_t(h, down_full, 1, 1).astype(BF) for h in hiddens]
    cot, hidden = jnp.concatenate(tie(cots, back), 0), jnp.concatenate(hiddens, 0)
    down_part = dot_t(cot, hidden, 0, 0).astype(BF)
    grad_ffn_in = jnp.concatenate(sums, 0)
    grad_h = own_cot + scale2 * gain_f * grad_ffn_in - hstate * scale2**3 * jnp.mean(
        grad_ffn_in * gain_f * hstate, -1, keepdims=True
    )
    own_low = grad_h.astype(BF)
    ffn_in, grad_gp = jnp.concatenate(tie(ins, back), 0), jnp.concatenate(tie(gps, back), 0)
    gate_part = dot_t(ffn_in, grad_gp, 0, 0).astype(BF)
    grad_up_pre = jnp.concatenate(tie(ups, back), 0)
    up_part = dot_t(ffn_in, grad_up_pre, 0, 0).astype(BF)
    own_back = dot_t(own_low, out_all, 1, 0).astype(BF)
    back_rows, rows_at = [own_back[:, :q_cols]], [z]
    for j in range(1, n_tensor):
        back_rows.append(ring(own_back[:, j * q_cols : (j + 1) * q_cols], TN, -j))
        rows_at.append((z + j) % n_tensor)
    grad_gated = place(back_rows, rows_at)

    def scattered(g):
        return lax.psum_scatter(g, ROWS, scatter_dimension=0, tiled=True).astype(F32)

    grad_down = scatter_rows(down_part)
    grad_gate, grad_up = scattered(gate_part), scattered(up_part)

    ffn_pieces = [
        jnp.concatenate([f[j * size : (j + 1) * size] for f in ffn_parts], 0)
        for j in range(n_tensor)
    ]
    layer_own = hstate + ring_sum(tie(ffn_pieces, back_rows))
    layer_out = lay_rows(ring_pieces(layer_own.astype(BF)), BF)[None]

    dq, dk, dv, gl = attend_back(
        q_rot, window, qkv, start, lse, grad_gated, attn_val, q_heads, kv_heads
    )
    out_part = dot_t(tie(own_low, dq), own_gated, 0, 0).astype(BF)

    def home(d):
        parts = [d[reach * rows :]]
        for k in range(1, reach + 1):
            parts.append(line(d[(reach - k) * rows : (reach - k + 1) * rows], CT, -k))
        return parts

    dks, dvs = home(dk), home(dv)
    out_sum = scattered(out_part).astype(BF)
    grad_out = out_sum[:, :q_cols].astype(F32)
    for j in range(1, n_tensor):
        grad_out = grad_out + ring(out_sum[:, j * q_cols : (j + 1) * q_cols], TN, -j).astype(F32)
    grad_pack, gain_sums = project_back(
        qkv, tie(dq, grad_gate), dks, dvs, gl, cos_t, sin_t, gain_q, gain_k, q_heads, kv_heads
    )
    attn_back = dot_t(grad_pack, pack, 1, 1).astype(BF)
    grad_attn_in = ring_sum([rows_of(attn_back, j) for j in range(n_tensor)])
    grad_attn_in = tie(grad_attn_in, grad_up)

    def spread(v):
        v = v.reshape(shards * chunks, query_gain.shape[0])
        return jnp.pad(v, ((0, 0), (0, block_rows - v.shape[1]))).reshape(width, 1)

    lane = lax.broadcasted_iota(jnp.int32, (1, pack.shape[1]), 1) - misc_at - q_heads
    extra = jnp.where(lane == 2, spread(gain_sums[0]), 0.0) + jnp.where(
        lane == 3, spread(gain_sums[1]), 0.0
    )
    pack_part = (dot_t(tie(attn_in, attn_back), grad_pack, 0, 0) + extra).astype(BF)
    weight_grad = scattered(pack_part)
    own_grad = grad_h + own_scale1 * gain_a * grad_attn_in - own_x * own_scale1**3 * jnp.mean(
        grad_attn_in * gain_a * own_x, -1, keepdims=True
    )

    def weighted(w, g):
        return jnp.sum(w.astype(F32) * g, 1)

    used = misc_at + q_heads
    small = jnp.stack(
        [
            weighted(packed[:, :used], weight_grad[:, :used]) / norm_attn.astype(F32),
            (weighted(w_gate, grad_gate) + weighted(w_up, grad_up)) / norm_ffn.astype(F32),
            weight_grad[:, used + 2],
            weight_grad[:, used + 3],
        ]
    )
    small = sum([ring(small, TN, k) for k in range(1, n_tensor)], small)

    own_pieces = ring_pieces(own_grad.astype(BF))
    tokens_grad = lay_rows(own_pieces, F32)[None]

    return (
        layer_out,
        tokens_grad,
        small[0],
        weight_grad[:, :q_cols],
        weight_grad[:, q_cols : q_cols + kv_cols],
        weight_grad[:, q_cols + kv_cols : misc_at],
        weight_grad[:, misc_at : misc_at + q_heads],
        small[2, : query_gain.shape[0]],
        small[3, : query_gain.shape[0]],
        grad_out,
        small[1],
        grad_gate,
        grad_up,
        grad_down,
    )


def solution(mesh):
    row = P((SH, CT))
    weight = P((SH, CT), TN)
    act = P(SH, CT, None)
    in_specs = (
        act, P(SH, CT), act, row, weight, weight, weight, weight, row, row, weight,
        row, weight, weight, weight,
    )
    out_specs = (
        act, act, row, weight, weight, weight, weight, row, row, weight, row, weight, weight,
        weight,
    )
    return jax.shard_map(
        per_device, mesh=mesh, in_specs=in_specs, out_specs=out_specs, check_vma=False
    )
```
